32 devices in a mesh: groups: 2 (over y), dp: 4 (over z), mp: 4 (over x, core).
Axes of the slice: x: 2, y: 2, z: 4, core: 2. Of those that a mesh axis runs over, the one named last changes fastest.
Arguments:
- tokens: bfloat16 [16384, 2048], P(('groups', 'dp'), 'mp'), parts along dimension 0, may hold values from -6 to 6
- x_weight: bfloat16 [2048, 2048], P(None, 'mp'), may hold values from -0.125 to 0.125
- z_weight: bfloat16 [2048, 2048], P(None, 'mp'), may hold values from -0.125 to 0.125
- bc_weight: bfloat16 [2048, 512], P(None, 'mp'), may hold values from -0.125 to 0.125
- dt_weight: bfloat16 [2048, 32], P(None, 'mp'), may hold values from -0.125 to 0.125
- dt_bias: float32 [32], P('mp'), may hold values from -3 to 1
- decay_rate: float32 [32], P('mp'), may hold values from 0.003 to 0.03
- norm_gain: float32 [2048], P('mp'), may hold values from 0.1 to 1.9
- out_weight: bfloat16 [2048, 2048], P('mp'), may hold values from -0.125 to 0.125
- store_states: bfloat16 [128, 131072], P(('groups', 'dp'), 'mp'), parts along dimension 0, may hold values from -6 to 6
- home_rows: int32 [128], P('groups'), parts along dimension 0, may hold values from 0 to 63, as said below
- event_counts: int32 [128], P(('groups', 'dp')), parts along dimension 0, may hold values from 1 to 128, as said below
Outputs:
- out_tokens: bfloat16 [16384, 2048], P(('groups', 'dp', 'mp')), parts along dimension 0
- new_store: bfloat16 [128, 131072], P(('groups', 'dp'), 'mp'), parts along dimension 0
The draws below stay inside these ranges and needn't reach their ends.
There are 2 independent parts, one for each index of `groups`. The reference program is written for one: setup_inputs(seed, part) draws one part's arguments, and reference() takes and returns one part's arrays. A program takes and returns all parts, laid end to end along the dimension named above; an argument that names none is the same for every part. Nothing has to cross between parts.
Inputs may be any that keep to these rules, and one draw needn't show every extreme that they name: A permutation: session r's state is row home_rows[r] of the store. The 16 sessions of one aligned block keep at most 4 states in one aligned block of 16 store rows, and every block of sessions reaches 4 in some block of rows. `event_counts`: event slots at or after a session's count are padding.
All inputs are finite; a program needn't handle non-finite values.
Results may differ from the reference program's by a relative error of at most 0.02.
Values may be sent and summed in bfloat16 or wider, within the bound.
A program may use at most 128 MiB of HBM per device.

```python
import math
import jax
import jax.numpy as jnp
from jax import lax

D = 2048
HEADS = 32
HEADDIM = 64
NSTATE = 64
GROUPS = 4
SPAN = 128
SES_DEV = 16
SESSIONS = 64
CAP = 4
INNER = 2048
N_DP = 4


def draw_home_rows(key, part):
    key_perm, key_fill, key_servers, key_store, key_place = jax.random.split(key, 5)
    lowest = max(1, (SES_DEV - N_DP + CAP - 2) // (CAP - 1))
    highest = SES_DEV // CAP
    full_pairs = jax.random.randint(key_fill, (), lowest, highest + 1)
    shard_order = jax.random.permutation(key_perm, N_DP)
    position = jnp.arange(SES_DEV, dtype=jnp.int32)
    paired = jnp.minimum(position // CAP, N_DP - 1)
    single = jnp.clip(full_pairs + position - full_pairs * CAP, 0, N_DP - 1)
    offset = shard_order[jnp.where(position < full_pairs * CAP, paired, single)]
    server_shift = jax.random.permutation(key_servers, N_DP)
    store_rotate = jax.random.randint(key_store, (N_DP,), 0, SES_DEV)
    place_rotate = jax.random.randint(key_place, (N_DP,), 0, SES_DEV)
    server = jnp.arange(N_DP, dtype=jnp.int32)[:, None]
    shard = (server_shift[server] + offset[None, :]) % N_DP
    slot = (position[None, :] + store_rotate[shard]) % SES_DEV
    place = (position[None, :] + place_rotate[server]) % SES_DEV
    target = (server * SES_DEV + place).reshape(-1)
    values = (shard * SES_DEV + slot).reshape(-1).astype(jnp.int32)
    return jnp.zeros((N_DP * SES_DEV,), jnp.int32).at[target].set(values)


def draw_event_counts(key, part):
    key_values, key_top, key_low = jax.random.split(key, 3)
    counts = jax.random.randint(key_values, (SESSIONS,), 1, SPAN + 1)
    top_index = jax.random.randint(key_top, (), 0, SESSIONS)
    low_index = (top_index + 1 + jax.random.randint(key_low, (), 0, SESSIONS - 1)) % SESSIONS
    counts = counts.at[top_index].set(SPAN)
    counts = counts.at[low_index].set(1)
    return counts.astype(jnp.int32)


def levels(own_key, dims, cuts, smallest, largest):
    def one(dim, parts):
        heights = jax.random.uniform(jax.random.fold_in(jax.random.fold_in(own_key, 6), dim), (parts,), jnp.float32, smallest / len(cuts), largest / len(cuts))
        return jnp.repeat(jnp.exp(heights), dims[dim] // parts).reshape((-1,) + (1,) * (len(dims) - dim - 1))

    factor_of = one(*cuts[0])
    for cut in cuts[1:]:
        factor_of = factor_of * one(*cut)
    return factor_of


def noise(rng, extent, width, bound, shards=(), kind=jnp.bfloat16):
    gain = levels(rng, extent, shards, -0.22, 0.18) if shards else 1.0
    result = jax.random.normal(rng, extent, jnp.float32) * width * gain
    return jnp.minimum(jnp.maximum(result, -bound), bound).astype(kind)


def setup_inputs(seed: int = 0, part: int = 0) -> dict:
    key_of = jax.random.split(jax.random.key(seed), 13)
    part_splits = jax.random.split(jax.random.fold_in(key_of[12], part), 13)
    tokens = noise(part_splits[0], (SESSIONS * SPAN, D), 1.0, 6.0, ((0, 4), (1, 4)))
    x_weight = noise(key_of[1], (D, INNER), D ** -0.5, 0.125, ((1, 4),))
    z_weight = noise(key_of[2], (D, INNER), D ** -0.5, 0.125, ((1, 4),))
    bc_weight = noise(key_of[3], (D, GROUPS * 2 * NSTATE), D ** -0.5, 0.125, ((1, 4),))
    dt_weight = noise(key_of[4], (D, HEADS), D ** -0.5, 0.125, ((1, 4),))
    dt_bias = jnp.clip(-3.0 + 4.0 * jax.random.uniform(key_of[5], (HEADS,), jnp.float32) ** levels(key_of[5], (HEADS,), ((0, 4),), -0.2, 0.2), -3.0, 1.0)
    decay_rate = jnp.clip(jnp.exp(math.log(0.03) - 2.3025851 * jax.random.uniform(key_of[6], (HEADS,), jnp.float32) ** levels(key_of[6], (HEADS,), ((0, 4),), -0.2, 0.2)), 0.003, 0.03)
    norm_gain = jnp.clip(1.0 + 0.18 * jax.random.normal(key_of[7], (INNER,), jnp.float32), 0.1, 1.9)
    out_weight = noise(key_of[8], (INNER, D), INNER ** -0.5, 0.125, ((0, 4),))
    store_states = noise(part_splits[9], (SESSIONS, HEADS * HEADDIM * NSTATE), 1.0, 6.0, ((0, 4), (1, 4)))
    home_rows = draw_home_rows(jax.random.fold_in(jax.random.fold_in(key_of[12], part), 71), part)
    event_counts = draw_event_counts(jax.random.fold_in(jax.random.fold_in(key_of[12], part), 71), part)
    return dict(tokens=tokens, x_weight=x_weight, z_weight=z_weight, bc_weight=bc_weight, dt_weight=dt_weight, dt_bias=dt_bias, decay_rate=decay_rate, norm_gain=norm_gain, out_weight=out_weight, store_states=store_states, home_rows=home_rows, event_counts=event_counts)


def rounded(values):
    return lax.optimization_barrier(values.astype(jnp.bfloat16)).astype(jnp.float32)

def group_scan(inputs, b_matrix, c_matrix, step_sizes, decay_rates, initial_state):
    decay_sum = jnp.cumsum(step_sizes * decay_rates[None, None, :], axis=1)
    causal_mask = jnp.arange(SPAN)[:, None] >= jnp.arange(SPAN)[None, :]
    lagged = jnp.transpose(decay_sum, (0, 2, 1))
    decay_gaps = jnp.where(causal_mask, lagged[:, :, :, None] - lagged[:, :, None, :], 0.0)
    kernel = jnp.einsum('stn,sun->stu', c_matrix, b_matrix)
    step_rows = jnp.transpose(step_sizes, (0, 2, 1))
    mixing = rounded(jnp.where(causal_mask, jnp.exp(-decay_gaps), 0.0) * step_rows[:, :, None, :] * kernel[:, None, :, :])
    diagonal_part = jnp.einsum('shtu,suhp->sthp', mixing, inputs)
    carried = jnp.einsum('stn,shpn->sthp', c_matrix, initial_state) * jnp.exp(-decay_sum)[:, :, :, None]
    final_decay = decay_sum[:, -1:, :]
    weighted = rounded(b_matrix[:, :, None, :] * (jnp.exp(-(final_decay - decay_sum)) * step_sizes)[:, :, :, None])
    new_state = jnp.exp(-final_decay[:, 0, :])[:, :, None, None] * initial_state + jnp.einsum('suhp,suhn->shpn', inputs, weighted)
    return (diagonal_part + carried, new_state)

def reference(tokens, x_weight, z_weight, bc_weight, dt_weight, dt_bias, decay_rate, norm_gain, out_weight, store_states, home_rows, event_counts):
    group_heads = HEADS // GROUPS
    group_width = group_heads * HEADDIM

    def one_block(block_index):
        first_row = (block_index * SES_DEV).astype(jnp.int32)
        token_rows = lax.dynamic_slice_in_dim(tokens, (first_row * SPAN).astype(jnp.int32), SES_DEV * SPAN, 0)
        wanted = lax.dynamic_slice_in_dim(home_rows, first_row, SES_DEV, 0)
        counts = lax.dynamic_slice_in_dim(event_counts, first_row, SES_DEV, 0)
        initial_all = jnp.take(store_states, wanted, axis=0).astype(jnp.float32).reshape(SES_DEV, HEADS, HEADDIM, NSTATE)
        inputs_all = rounded(jnp.dot(token_rows, x_weight, preferred_element_type=jnp.float32)).reshape(SES_DEV, SPAN, HEADS, HEADDIM)
        gate_values = rounded(jnp.dot(token_rows, z_weight, preferred_element_type=jnp.float32)).reshape(SES_DEV, SPAN, INNER)
        bc_values = rounded(jnp.dot(token_rows, bc_weight, preferred_element_type=jnp.float32)).reshape(SES_DEV, SPAN, GROUPS, 2, NSTATE)
        valid_mask = (jnp.arange(SPAN, dtype=jnp.int32)[None, :] < counts[:, None]).astype(jnp.float32)
        raw_steps = jnp.dot(token_rows, dt_weight, preferred_element_type=jnp.float32).reshape(SES_DEV, SPAN, HEADS)
        step_sizes = jax.nn.softplus(raw_steps + dt_bias[None, None, :]) * valid_mask[:, :, None]
        pieces_out = []
        pieces_state = []
        for group_index in range(GROUPS):
            head_range = slice(group_index * group_heads, (group_index + 1) * group_heads)
            outputs, new_state = group_scan(inputs_all[:, :, head_range], bc_values[:, :, group_index, 0], bc_values[:, :, group_index, 1], step_sizes[:, :, head_range], decay_rate[head_range], initial_all[:, head_range])
            channel_range = slice(group_index * group_width, (group_index + 1) * group_width)
            gated_values = outputs.reshape(SES_DEV, SPAN, group_width) * jax.nn.silu(gate_values[:, :, channel_range])
            inverse_rms = lax.rsqrt(lax.optimization_barrier(jnp.mean(gated_values * gated_values, axis=2, keepdims=True)) + 1e-05)
            pieces_out.append(gated_values * inverse_rms * norm_gain[channel_range][None, None, :] * valid_mask[:, :, None])
            pieces_state.append(new_state)
        normed = jnp.concatenate(pieces_out, axis=2).reshape(SES_DEV * SPAN, INNER).astype(jnp.bfloat16)
        out_block = jnp.dot(normed, out_weight, preferred_element_type=jnp.float32).astype(jnp.bfloat16)
        states_block = jnp.concatenate(pieces_state, axis=1).astype(jnp.bfloat16).reshape(SES_DEV, HEADS * HEADDIM * NSTATE)
        return (out_block, states_block)
    out_blocks, state_blocks = lax.map(one_block, jnp.arange(SESSIONS // SES_DEV, dtype=jnp.int32))
    out_tokens = out_blocks.reshape(SESSIONS * SPAN, D)
    new_store = jnp.zeros_like(store_states).at[home_rows].set(state_blocks.reshape(SESSIONS, HEADS * HEADDIM * NSTATE))
    return (out_tokens, new_store)
```

```python
import functools

import jax
import jax.numpy as jnp
from jax import lax
from jax.experimental import pallas as pl
from jax.experimental.pallas import tpu as pltpu
from jax.sharding import PartitionSpec as P

F32 = jnp.float32
BF16 = jnp.bfloat16
MESH = pl.DeviceIdType.MESH


def xor_place(me, mask):
    return lax.rem(lax.rem(me, 2) + mask % 2, 2) + 2 * lax.rem(me // 2 + mask // 2, 2)


def wrap(value, size):
    return jnp.where(value >= size, value - size, value)


def slot_tables(home, dp, sessions, shards, capacity):
    total = home.shape[1]
    base = (dp * sessions).astype(F32)
    here = dp.astype(F32)
    home = home.astype(F32)
    who = lax.broadcasted_iota(jnp.int32, (sessions, total), 1).astype(F32)
    spot = lax.broadcasted_iota(jnp.int32, (sessions, total), 0).astype(F32) + base
    owner = jnp.sum(jnp.where(home == spot, who, 0.0), axis=1, keepdims=True)
    wanted = jnp.sum(jnp.where(who == spot, home, 0.0), axis=1, keepdims=True)
    server = jnp.floor(owner * (1.0 / sessions))
    shard = jnp.floor(wanted * (1.0 / sessions))
    place = lax.broadcasted_iota(jnp.int32, (sessions, 128), 0).astype(F32)
    lane = lax.broadcasted_iota(jnp.int32, (sessions, 128), 1).astype(F32)

    def as_row(column):
        return jnp.sum(jnp.where(place == lane, column, 0.0), axis=0, keepdims=True)

    def rank(keys, order):
        earlier = (as_row(keys) == keys) & (as_row(order) < order) & (lane < sessions)
        return jnp.sum(jnp.where(earlier, 1.0, 0.0), axis=1, keepdims=True)

    to_server = wrap(server - here + shards, shards)
    from_home = wrap(here - shard + shards, shards)
    row_slot = to_server * capacity + rank(server, place[:, :1])
    session_slot = from_home * capacity + rank(shard, wanted - shard * sessions)

    def holder(slots):
        return jnp.sum(jnp.where(slots == lane, place, 0.0), axis=0, keepdims=True)

    rows = [as_row(session_slot), as_row(row_slot), holder(row_slot), holder(session_slot)]
    return jnp.concatenate(rows + [jnp.zeros((4, 128), F32)], axis=0).astype(jnp.int32)


def layer_kernel(
    heads,
    head_size,
    state_size,
    chunks,
    parts,
    shards,
    share,
    capacity,
    counts,
    home_hbm,
    tokens_hbm,
    store_hbm,
    x_hbm,
    z_hbm,
    bc_hbm,
    dtw_ref,
    bias_ref,
    rate_ref,
    gain_ref,
    outw_hbm,
    out_hbm,
    new_store_hbm,
    x_ref,
    z_ref,
    bd_ref,
    outw,
    tok,
    home_ref,
    table_ref,
    table,
    raw_store,
    store_ref,
    outbound,
    inbound,
    state_ref,
    outgoing,
    returned,
    xs_ref,
    zs_ref,
    bc_ref,
    dt_ref,
    normed,
    got,
    sums,
    out_ref,
    load_sem,
    table_sem,
    own_sem,
    sib_send,
    sib_recv,
    far_send,
    far_recv,
    diag_send,
    diag_recv,
    store_send,
    store_recv,
    back_send,
    back_recv,
    piece_send,
    piece_recv,
    spread_send,
    spread_recv,
    across_send,
    across_recv,
    pass_send,
    pass_recv,
    norm_send,
    norm_recv,
    write_sem,
):
    slots = tokens_hbm.shape[2]
    depth = tokens_hbm.shape[3]
    model = outw_hbm.shape[1]
    inner = heads * head_size
    sessions = chunks * parts
    rounds = 2 * chunks
    lag = rounds // 2
    rows = 2 * slots
    me = lax.axis_index("mp")
    dp = lax.axis_index("dp")
    group = lax.axis_index("groups")
    half = lax.rem(me, 2)
    side = me // 2
    low = lax.rem(dp, share)
    pieces = 2 * share
    height = inner // pieces
    sib_id = {"mp": xor_place(me, 1)}
    far_id = {"mp": xor_place(me, 2)}
    diag_id = {"mp": xor_place(me, 3)}
    other_id = {"groups": 1 - group}

    def look(line, at, size):
        return jnp.minimum(jnp.maximum(table[line, at], 0), size - 1)

    loads = [
        pltpu.make_async_copy(home_hbm, home_ref, load_sem.at[0]),
        pltpu.make_async_copy(store_hbm, raw_store, load_sem.at[1]),
        pltpu.make_async_copy(outw_hbm, outw.at[0], load_sem.at[2]),
    ]
    for s in range(parts):
        part = pl.ds(pl.multiple_of(xor_place(me, s) * depth, depth), depth)
        there = pl.ds(s * depth, depth)
        loads.append(pltpu.make_async_copy(x_hbm.at[part], x_ref.at[there], load_sem.at[3 + 3 * s]))
        loads.append(pltpu.make_async_copy(z_hbm.at[part], z_ref.at[there], load_sem.at[4 + 3 * s]))
        loads.append(
            pltpu.make_async_copy(
                bc_hbm.at[part], bd_ref.at[there, pl.ds(0, 2 * state_size)], load_sem.at[5 + 3 * s]
            )
        )
    for load in loads:
        load.start()

    barrier = pltpu.get_barrier_semaphore()
    for mask in range(1, parts):
        pl.semaphore_signal(
            barrier, inc=1, device_id={"mp": xor_place(me, mask)}, device_id_type=MESH
        )
    for k in range(1, shards):
        pl.semaphore_signal(
            barrier, inc=1, device_id={"dp": lax.rem(dp + k, shards)}, device_id_type=MESH
        )
    pl.semaphore_signal(barrier, inc=1, device_id=other_id, device_id_type=MESH)
    pl.semaphore_wait(barrier, parts - 1 + shards - 1 + 1)

    def remote(src, dst, send, recv, device):
        return pltpu.make_async_remote_copy(
            src_ref=src,
            dst_ref=dst,
            send_sem=send,
            recv_sem=recv,
            device_id=device,
            device_id_type=MESH,
        )

    def owners(q, side):
        return lax.rem(1 + side + q // chunks, 2)

    def token_rows(q, side):
        return tokens_hbm.at[pl.ds(2 * owners(q, side), 2), lax.rem(q, chunks)]

    def columns(s):
        return pl.ds(s * depth, depth)

    def own_copy(q):
        return pltpu.make_async_copy(
            token_rows(q, side), tok.at[q, :, :, columns(0)], own_sem.at[q]
        )

    def sib_copy(q):
        return remote(
            token_rows(q, side), tok.at[q, :, :, columns(1)], sib_send.at[q], sib_recv.at[q], sib_id
        )

    def far_copy(q):
        return remote(
            token_rows(q, 1 - side),
            tok.at[q, :, :, columns(2)],
            far_send.at[q],
            far_recv.at[q],
            far_id,
        )

    def diag_copy(q):
        return remote(
            tok.at[q, :, :, columns(2)],
            tok.at[q, :, :, columns(3)],
            diag_send.at[q],
            diag_recv.at[q],
            sib_id,
        )

    def store_copy(k):
        return remote(
            outbound.at[pl.ds(k * capacity, capacity)],
            inbound.at[pl.ds(k * capacity, capacity)],
            store_send.at[k],
            store_recv.at[k],
            {"dp": lax.rem(dp + k, shards)},
        )

    def back_copy(k):
        return remote(
            outgoing.at[pl.ds(k * capacity, capacity)],
            returned.at[pl.ds(k * capacity, capacity)],
            back_send.at[k],
            back_recv.at[k],
            {"dp": lax.rem(dp + shards - k, shards)},
        )

    def piece_at(g, k):
        return pl.ds(pl.multiple_of((g * share + k) * height, height), height)

    def near(k):
        return lax.rem(low + k, share)

    def piece_copy():
        here = piece_at(group, low)
        return remote(outw.at[0, here], outw.at[2, here], piece_send, piece_recv, far_id)

    def spread_copy(k):
        here = piece_at(group, low)
        return remote(
            outw.at[2, here],
            outw.at[2, here],
            spread_send.at[k],
            spread_recv.at[k],
            {"dp": dp - low + near(k)},
        )

    def across_copy(k):
        here = piece_at(group, near(k))
        return remote(
            outw.at[2, here], outw.at[2, here], across_send.at[k], across_recv.at[k], other_id
        )

    def pass_copy(g, k):
        here = piece_at(g, k)
        n = g * share + k
        return remote(outw.at[2, here], outw.at[3, here], pass_send.at[n], pass_recv.at[n], sib_id)

    def whole_copy():
        n = pieces
        return remote(outw.at[0], outw.at[1], pass_send.at[n], pass_recv.at[n], sib_id)

    def norm_copy(s, j):
        if s == 1:
            t, device = 2 * (chunks + j) + 1 - half, sib_id
        elif s == 2:
            t, device = 2 * j + half, far_id
        else:
            t, device = 2 * j + 1 - half, diag_id
        return remote(
            normed.at[t], got.at[s - 1, j], norm_send.at[s - 1, j], norm_recv.at[s - 1, j], device
        )

    ahead = min(3, rounds)
    for q in range(ahead):
        far_copy(q).start()

    loads[0].wait()
    table_ref[...] = slot_tables(home_ref[...], dp, sessions, shards, capacity)
    table_copy = pltpu.make_async_copy(table_ref, table, table_sem)
    table_copy.start()

    @pl.loop(0, rounds)
    def _(q):
        own_copy(q).start()
        sib_copy(q).start()

    lane = lax.broadcasted_iota(jnp.int32, (slots, slots), 1)
    row = lax.broadcasted_iota(jnp.int32, (slots, slots), 0)
    pair = 2 * head_size
    wide = 256
    tall = lax.broadcasted_iota(jnp.int32, (wide, wide), 0)
    flat = lax.broadcasted_iota(jnp.int32, (wide, wide), 1)
    band = wide // sessions
    swap_in = (flat == lax.rem(tall, band) * sessions + tall // band).astype(BF16)
    swap_out = (flat == lax.rem(tall, sessions) * band + tall // sessions).astype(BF16)
    blocks = store_ref.shape[1] // band

    loads[1].wait()

    @pl.loop(0, blocks)
    def _(b):
        base = b * (band * 128)
        stacked = jnp.concatenate(
            [
                raw_store[:, pl.ds(pl.multiple_of(base + a * 128, 128), 128)]
                for a in range(band)
            ],
            axis=0,
        )
        moved = jnp.dot(swap_in, stacked, preferred_element_type=F32).astype(BF16)
        at = pl.ds(pl.multiple_of(b * band, band), band)
        store_ref[:, at, :] = moved.reshape(sessions, band, 128)

    table_copy.wait()
    for k in range(1, shards):
        for c in range(capacity):
            outbound[k * capacity + c] = store_ref[look(2, k * capacity + c, sessions)]
        store_copy(k).start()
    for c in range(capacity):
        inbound[c] = store_ref[look(2, c, sessions)]

    within = lax.rem(lane, head_size)
    first = within < head_size // 2
    places = row == 2 * within + lane // head_size
    spread = places.astype(BF16)
    back = (lane == 2 * lax.rem(row, head_size) + row // head_size).astype(BF16)
    tile = min(512, model)

    loads[2].wait()

    @pl.loop(0, model // tile)
    def _(t):
        cols = pl.ds(pl.multiple_of(t * tile, tile), tile)
        for g in range(heads // 2):
            part = slice(g * pair, (g + 1) * pair)
            moved = jnp.dot(back, outw[0, part, cols], preferred_element_type=F32)
            outw[0, part, cols] = moved.astype(BF16)

    piece_copy().start()
    whole_copy().start()

    eye = lax.broadcasted_iota(jnp.int32, (heads, heads), 0) == lax.broadcasted_iota(
        jnp.int32, (heads, heads), 1
    )
    rate_col = jnp.sum(jnp.where(eye, rate_ref[...], 0.0), axis=1, keepdims=True)
    bias_col = jnp.sum(jnp.where(eye, bias_ref[...], 0.0), axis=1, keepdims=True)
    causal = row >= lane
    lane8 = lax.broadcasted_iota(jnp.int32, (heads, slots), 1)
    gains = []
    for g in range(heads // 2):
        column = jnp.sum(
            jnp.where(row == lane, gain_ref[:, g * pair : (g + 1) * pair], 0.0),
            axis=1,
            keepdims=True,
        )
        gains.append(jnp.sum(jnp.where(places, column, 0.0), axis=0, keepdims=True))

    for load in loads[3:]:
        load.wait()

    for s in range(parts):
        start = xor_place(me, s) * depth
        for b in range(depth // 128):
            cut = dtw_ref[:, pl.ds(pl.multiple_of(start + b * 128, 128), 128)].astype(F32)
            cut = jnp.concatenate([cut, jnp.zeros((128 - heads, 128), F32)], axis=0)
            at = slice(s * depth + b * 128, s * depth + (b + 1) * 128)
            bd_ref[at, 2 * state_size :] = cut.T.astype(BF16)

    @pl.loop(0, parts)
    def _(t):
        part = pl.ds(pl.multiple_of(t * depth, depth), depth)
        for ref in (x_ref, z_ref):
            for g in range(heads // 2):
                cols = slice(g * pair, (g + 1) * pair)
                moved = jnp.dot(ref[part, cols], spread, preferred_element_type=F32)
                ref[part, cols] = moved.astype(BF16)

    def session(q, o):
        t = 2 * q + o
        index = (2 * owners(q, side) + o) * chunks + lax.rem(q, chunks)
        count = counts[index]
        spot = look(0, index, shards * capacity)
        b_bf = bc_ref[t, :, :state_size]
        b_f32 = b_bf.astype(F32)
        c_bf = bc_ref[t, :, state_size:]
        raw = dt_ref[t].T[:heads, :] + bias_col
        dt_t = jnp.maximum(raw, 0.0) + jnp.log1p(jnp.exp(-jnp.abs(raw)))
        dt_t = jnp.where(lane8 < count, dt_t, 0.0)
        cum_t = dt_t * rate_col
        shift = 1
        while shift < slots:
            moved = pltpu.roll(cum_t, shift, axis=1)
            cum_t = cum_t + jnp.where(lane8 >= shift, moved, 0.0)
            shift *= 2
        last = cum_t[:, slots - 1 : slots]
        weigh_t = jnp.exp(cum_t - last) * dt_t
        fade_t = jnp.exp(-cum_t)
        stacked = jnp.concatenate(
            [cum_t, weigh_t, fade_t, jnp.zeros((slots - 3 * heads, slots), F32)], axis=0
        ).T
        scores = lax.dot_general(
            c_bf, b_bf, (((1,), (1,)), ((), ())), preferred_element_type=F32
        )
        gated_parts = []
        squares = None
        for g in range(heads // 2):
            cols = slice(g * pair, (g + 1) * pair)
            xs = xs_ref[t, :, cols]
            zs = zs_ref[t, :, cols].astype(F32)
            split = jnp.concatenate(
                [jnp.where(first, xs, jnp.zeros((), BF16)), jnp.where(first, jnp.zeros((), BF16), xs)],
                axis=0,
            )
            mixes = []
            weighed = []
            for h in (2 * g, 2 * g + 1):
                gaps = jnp.where(causal, cum_t[h : h + 1, :] - stacked[:, h : h + 1], -1e30)
                mixes.append((jnp.exp(gaps) * dt_t[h : h + 1, :] * scores).astype(BF16))
                weighed.append((b_f32 * stacked[:, heads + h : heads + h + 1]).astype(BF16))
            y = jnp.dot(jnp.concatenate(mixes, axis=1), split, preferred_element_type=F32)
            part = slice(g * head_size, (g + 1) * head_size)
            kept = inbound[spot, part, :]
            halves = jnp.concatenate([kept[:, :state_size], kept[:, state_size:]], axis=0)
            carried = lax.dot_general(
                c_bf, halves, (((1,), (1,)), ((), ())), preferred_element_type=F32
            )
            fade0 = stacked[:, 2 * heads + 2 * g : 2 * heads + 2 * g + 1]
            fade1 = stacked[:, 2 * heads + 2 * g + 1 : 2 * heads + 2 * g + 2]
            y = y + carried * jnp.where(first, fade0, fade1)
            grown = lax.dot_general(
                split,
                jnp.concatenate(weighed, axis=0),
                (((0,), (0,)), ((), ())),
                preferred_element_type=F32,
            )
            keep = jnp.where(
                row[:head_size] < head_size // 2,
                fade_t[2 * g : 2 * g + 1, slots - 1 : slots],
                fade_t[2 * g + 1 : 2 * g + 2, slots - 1 : slots],
            )
            grown = jnp.concatenate([grown[:head_size], grown[head_size:]], axis=1)
            state_ref[index, part, :] = (keep * kept.astype(F32) + grown).astype(BF16)
            gated = y * (zs * jax.nn.sigmoid(zs))
            square = jnp.sum(gated * gated, axis=1, keepdims=True)
            squares = square if squares is None else squares + square
            gated_parts.append(gated)
        scale = lax.rsqrt(squares * (1.0 / inner) + 1e-05)
        scale = jnp.where(row[:, :1] < count, scale, 0.0)
        for g in range(heads // 2):
            cols = slice(g * pair, (g + 1) * pair)
            normed[t, :, cols] = (gated_parts[g] * scale * gains[g]).astype(BF16)

    def project(q):
        own_copy(q).wait()
        sib_copy(q).wait_recv()
        diag_copy(q).wait_recv()
        values = tok[q].reshape(rows, parts * depth)
        at = pl.ds(2 * q, 2)
        for weight, ref in ((x_ref, xs_ref), (z_ref, zs_ref)):
            total = jnp.dot(values, weight[...], preferred_element_type=F32)
            ref[at] = total.astype(BF16).reshape(2, slots, inner)
        total = jnp.dot(values, bd_ref[...], preferred_element_type=F32)
        bc_ref[at] = total[:, : 2 * state_size].astype(BF16).reshape(2, slots, 2 * state_size)
        dt_ref[at] = total[:, 2 * state_size :].reshape(2, slots, 128)

    def reached(q):
        return jnp.where(q < lag, 0, jnp.minimum(jnp.minimum(2 * (q - lag + 1), q), rounds))

    def round_trip(q, carry):
        @pl.when(q < rounds)
        def _():
            far_copy(q).wait_recv()
            diag_copy(q).start()

        @pl.when(q + ahead < rounds)
        def _():
            far_copy(q + ahead).start()

        @pl.when(q == 1)
        def _():
            piece_copy().wait_recv()
            across_copy(0).start()
            pass_copy(group, low).start()

        @pl.when(q == lag)
        def _():
            for k in range(1, shards):
                store_copy(k).wait_recv()
            for k in range(1, share):
                spread_copy(k).start()

        @pl.when(q == rounds - 1)
        def _():
            for j in range(chunks):
                norm_copy(2, j).start()
                norm_copy(3, j).start()

        @pl.loop(reached(q - 1), reached(q))
        def _(done):
            session(done, 0)
            session(done, 1)

        @pl.when(q < rounds)
        def _():
            project(q)

        return carry

    lax.fori_loop(0, rounds + 1, round_trip, 0)

    for k in range(1, shards):
        for c in range(capacity):
            outgoing[k * capacity + c] = state_ref[look(3, k * capacity + c, sessions)]
        back_copy(k).start()
    for j in range(chunks):
        norm_copy(1, j).start()
    for k in range(1, share):
        spread_copy(k).wait_recv()
        across_copy(share - k).start()
        pass_copy(group, near(share - k)).start()
    for c in range(capacity):
        returned[c] = state_ref[look(3, c, sessions)]

    whole_copy().wait_recv()
    for j in range(chunks):
        norm_copy(1, j).wait_recv()

    @pl.loop(0, model // tile)
    def _(t):
        cols = pl.ds(pl.multiple_of(t * tile, tile), tile)
        for j in range(chunks):
            mine = normed[2 * (chunks + j) + half]
            total = jnp.dot(mine, outw[0, :, cols], preferred_element_type=F32)
            total += jnp.dot(got[0, j], outw[1, :, cols], preferred_element_type=F32)
            sums[j, :, cols] = total

    for k in range(share):
        across_copy(k).wait_recv()
        pass_copy(1 - group, near(k)).start()
    for k in range(share):
        pass_copy(group, near(k)).wait_recv()
        pass_copy(1 - group, near(k)).wait_recv()

    writes = []
    for j in range(chunks):
        norm_copy(2, j).wait_recv()
        norm_copy(3, j).wait_recv()

        @pl.loop(0, model // tile)
        def _(t):
            cols = pl.ds(pl.multiple_of(t * tile, tile), tile)
            total = sums[j, :, cols]
            for s in (2, 3):
                total += jnp.dot(got[s - 1, j], outw[s, :, cols], preferred_element_type=F32)
            out_ref[j, :, cols] = total.astype(BF16)

        writes.append(
            pltpu.make_async_copy(
                out_ref.at[j], out_hbm.at[pl.ds(j * slots, slots)], write_sem.at[j]
            )
        )
        writes[-1].start()

    for k in range(1, shards):
        back_copy(k).wait_recv()

    @pl.loop(0, blocks)
    def _(b):
        at = pl.ds(pl.multiple_of(b * band, band), band)
        stacked = jnp.concatenate([returned[look(1, r, shards * capacity), at, :] for r in range(sessions)], axis=0)
        moved = jnp.dot(swap_out, stacked, preferred_element_type=F32).astype(BF16)
        base = b * (band * 128)
        for a in range(band):
            raw_store[:, pl.ds(pl.multiple_of(base + a * 128, 128), 128)] = moved[
                a * sessions : (a + 1) * sessions
            ]

    writes.append(pltpu.make_async_copy(raw_store, new_store_hbm, write_sem.at[chunks]))
    writes[-1].start()

    @pl.loop(0, rounds)
    def _(q):
        far_copy(q).wait_send()
        sib_copy(q).wait_send()
        diag_copy(q).wait_send()

    for j in range(chunks):
        for s in range(1, parts):
            norm_copy(s, j).wait_send()
    for k in range(1, shards):
        store_copy(k).wait_send()
        back_copy(k).wait_send()
    piece_copy().wait_send()
    whole_copy().wait_send()
    for k in range(share):
        if k:
            spread_copy(k).wait_send()
        across_copy(k).wait_send()
        pass_copy(0, k).wait_send()
        pass_copy(1, k).wait_send()
    for write in writes:
        write.wait()


def run_layer(counts, home, tokens4, store, weights, params, out_weight, sizes, shards, capacity):
    heads, head_size, state_size = sizes
    parts, chunks, slots, depth = tokens4.shape
    x_weight, z_weight, bc_weight, dt_weight = weights
    inner = heads * head_size
    model = out_weight.shape[1]
    sessions, state_width = store.shape
    share = min(4, shards)
    pieces = 2 * share
    rounds = 2 * chunks
    vmem = pl.BlockSpec(memory_space=pltpu.VMEM)
    hbm = pl.BlockSpec(memory_space=pl.ANY)
    dma = pltpu.SemaphoreType.DMA
    state = (state_width // 128, 128)
    exchange = pltpu.VMEM((shards * capacity,) + state, BF16)
    kept = pltpu.VMEM((sessions,) + state, BF16)
    width = parts * depth
    return pl.pallas_call(
        functools.partial(
            layer_kernel, heads, head_size, state_size, chunks, parts, shards, share, capacity
        ),
        out_shape=(
            jax.ShapeDtypeStruct((chunks * slots, model), BF16),
            jax.ShapeDtypeStruct(store.shape, BF16),
        ),
        in_specs=[pl.BlockSpec(memory_space=pltpu.SMEM)] + [hbm] * 6 + [vmem] * 4 + [hbm],
        out_specs=(hbm, hbm),
        scratch_shapes=[
            pltpu.VMEM((width, inner), BF16),
            pltpu.VMEM((width, inner), BF16),
            pltpu.VMEM((width, 2 * state_size + 128), BF16),
            pltpu.VMEM((parts, inner, model), BF16),
            pltpu.VMEM((rounds, 2, slots, width), BF16),
            pltpu.VMEM(home.shape, jnp.int32),
            pltpu.VMEM((8, 128), jnp.int32),
            pltpu.SMEM((8, 128), jnp.int32),
            pltpu.VMEM(store.shape, BF16),
            kept,
            exchange,
            exchange,
            kept,
            exchange,
            exchange,
            pltpu.VMEM((sessions, slots, inner), BF16),
            pltpu.VMEM((sessions, slots, inner), BF16),
            pltpu.VMEM((sessions, slots, 2 * state_size), BF16),
            pltpu.VMEM((sessions, slots, 128), F32),
            pltpu.VMEM((sessions, slots, inner), BF16),
            pltpu.VMEM((parts - 1, chunks, slots, inner), BF16),
            pltpu.VMEM((chunks, slots, model), F32),
            pltpu.VMEM((chunks, slots, model), BF16),
            dma((3 + 3 * parts,)),
            dma,
        ]
        + [dma((rounds,))] * 7
        + [dma((shards,))] * 4
        + [dma, dma]
        + [dma((share,))] * 4
        + [dma((pieces + 1,))] * 2
        + [dma((parts - 1, chunks))] * 2
        + [dma((chunks + 1,))],
        compiler_params=pltpu.CompilerParams(
            vmem_limit_bytes=62 * 1024 * 1024, collective_id=0, has_side_effects=True
        ),
        cost_estimate=pl.CostEstimate(
            flops=2 * sessions * slots * width * (2 * inner + 256 + model // parts),
            bytes_accessed=16 * 1024 * 1024,
            transcendentals=sessions * slots * heads * slots,
        ),
        name="layer",
    )(
        counts,
        home,
        tokens4,
        store,
        x_weight,
        z_weight,
        bc_weight,
        dt_weight.T,
        *params,
        out_weight,
    )


def body(
    tokens,
    x_weight,
    z_weight,
    bc_weight,
    dt_weight,
    dt_bias,
    decay_rate,
    norm_gain,
    out_weight,
    store_states,
    home_rows,
    event_counts,
):
    shards = lax.axis_size("dp")
    parts = lax.axis_size("mp")
    sessions = store_states.shape[0]
    capacity = max(2, (sessions + shards - 1) // shards)
    heads = dt_bias.shape[0]
    inner = x_weight.shape[1]
    state_size = bc_weight.shape[1] // 2
    slots = tokens.shape[0] // sessions
    tokens4 = tokens.reshape(parts, sessions // parts, slots, tokens.shape[1])
    return run_layer(
        event_counts,
        home_rows[None, :],
        tokens4,
        store_states,
        (x_weight, z_weight, bc_weight, dt_weight),
        (dt_bias[None, :], decay_rate[None, :], norm_gain[None, :]),
        out_weight,
        (heads, inner // heads, state_size),
        shards,
        capacity,
    )


def solution(mesh):
    return jax.shard_map(
        body,
        mesh=mesh,
        in_specs=(
            P(("groups", "dp"), "mp"),
            P(None, "mp"),
            P(None, "mp"),
            P(None, "mp"),
            P(None, "mp"),
            P("mp"),
            P("mp"),
            P("mp"),
            P("mp", None),
            P(("groups", "dp"), "mp"),
            P("groups"),
            P(("groups", "dp")),
        ),
        out_specs=(P(("groups", "dp", "mp"), None), P(("groups", "dp"), "mp")),
        check_vma=False,
    )
```

```python
import functools

import jax
import jax.numpy as jnp
from jax import lax
from jax.experimental import pallas as pl
from jax.experimental.pallas import tpu as pltpu
from jax.sharding import PartitionSpec as P

F32 = jnp.float32
BF16 = jnp.bfloat16
MESH = pl.DeviceIdType.MESH


def xor_place(me, mask):
    return lax.rem(lax.rem(me, 2) + mask % 2, 2) + 2 * lax.rem(me // 2 + mask // 2, 2)


def wrap(value, size):
    return jnp.where(value >= size, value - size, value)


def slot_tables(home, dp, sessions, shards, capacity):
    total = home.shape[1]
    base = (dp * sessions).astype(F32)
    here = dp.astype(F32)
    home = home.astype(F32)
    who = lax.broadcasted_iota(jnp.int32, (sessions, total), 1).astype(F32)
    spot = lax.broadcasted_iota(jnp.int32, (sessions, total), 0).astype(F32) + base
    owner = jnp.sum(jnp.where(home == spot, who, 0.0), axis=1, keepdims=True)
    wanted = jnp.sum(jnp.where(who == spot, home, 0.0), axis=1, keepdims=True)
    server = jnp.floor(owner * (1.0 / sessions))
    shard = jnp.floor(wanted * (1.0 / sessions))
    place = lax.broadcasted_iota(jnp.int32, (sessions, 128), 0).astype(F32)
    lane = lax.broadcasted_iota(jnp.int32, (sessions, 128), 1).astype(F32)

    def as_row(column):
        return jnp.sum(jnp.where(place == lane, column, 0.0), axis=0, keepdims=True)

    def rank(keys, order):
        earlier = (as_row(keys) == keys) & (as_row(order) < order) & (lane < sessions)
        return jnp.sum(jnp.where(earlier, 1.0, 0.0), axis=1, keepdims=True)

    to_server = wrap(server - here + shards, shards)
    from_home = wrap(here - shard + shards, shards)
    row_slot = to_server * capacity + rank(server, place[:, :1])
    session_slot = from_home * capacity + rank(shard, wanted - shard * sessions)

    def holder(slots):
        return jnp.sum(jnp.where(slots == lane, place, 0.0), axis=0, keepdims=True)

    rows = [as_row(session_slot), as_row(row_slot), holder(row_slot), holder(session_slot)]
    return jnp.concatenate(rows + [jnp.zeros((4, 128), F32)], axis=0).astype(jnp.int32)


def layer_kernel(
    heads,
    head_size,
    state_size,
    chunks,
    parts,
    shards,
    share,
    capacity,
    counts,
    home_hbm,
    tokens_hbm,
    store_hbm,
    x_hbm,
    z_hbm,
    bc_hbm,
    dtw_ref,
    bias_ref,
    rate_ref,
    gain_ref,
    outw_hbm,
    out_hbm,
    new_store_hbm,
    x_ref,
    z_ref,
    bd_ref,
    outw,
    tok,
    home_ref,
    table_ref,
    table,
    raw_store,
    store_ref,
    outbound,
    inbound,
    state_ref,
    outgoing,
    returned,
    xs_ref,
    zs_ref,
    bc_ref,
    rows_ref,
    cols_ref,
    pick_ref,
    normed,
    got,
    sums,
    out_ref,
    load_sem,
    table_sem,
    own_sem,
    sib_send,
    sib_recv,
    far_send,
    far_recv,
    diag_send,
    diag_recv,
    store_send,
    store_recv,
    back_send,
    back_recv,
    piece_send,
    piece_recv,
    spread_send,
    spread_recv,
    across_send,
    across_recv,
    pass_send,
    pass_recv,
    norm_send,
    norm_recv,
    write_sem,
):
    slots = tokens_hbm.shape[2]
    depth = tokens_hbm.shape[3]
    model = outw_hbm.shape[1]
    inner = heads * head_size
    sessions = chunks * parts
    rounds = 2 * chunks
    lag = rounds // 2
    rows = 2 * slots
    me = lax.axis_index("mp")
    dp = lax.axis_index("dp")
    group = lax.axis_index("groups")
    half = lax.rem(me, 2)
    side = me // 2
    low = lax.rem(dp, share)
    pieces = 2 * share
    height = inner // pieces
    sib_id = {"mp": xor_place(me, 1)}
    far_id = {"mp": xor_place(me, 2)}
    diag_id = {"mp": xor_place(me, 3)}
    other_id = {"groups": 1 - group}

    def look(line, at, size):
        return jnp.minimum(jnp.maximum(table[line, at], 0), size - 1)

    loads = [
        pltpu.make_async_copy(home_hbm, home_ref, load_sem.at[0]),
        pltpu.make_async_copy(store_hbm, raw_store, load_sem.at[1]),
        pltpu.make_async_copy(outw_hbm, outw.at[0], load_sem.at[2]),
    ]
    for s in range(parts):
        part = pl.ds(pl.multiple_of(xor_place(me, s) * depth, depth), depth)
        there = pl.ds(s * depth, depth)
        loads.append(pltpu.make_async_copy(x_hbm.at[part], x_ref.at[there], load_sem.at[3 + 3 * s]))
        loads.append(pltpu.make_async_copy(z_hbm.at[part], z_ref.at[there], load_sem.at[4 + 3 * s]))
        loads.append(
            pltpu.make_async_copy(
                bc_hbm.at[part], bd_ref.at[there, pl.ds(0, 2 * state_size)], load_sem.at[5 + 3 * s]
            )
        )
    for load in loads:
        load.start()

    barrier = pltpu.get_barrier_semaphore()
    for mask in range(1, parts):
        pl.semaphore_signal(
            barrier, inc=1, device_id={"mp": xor_place(me, mask)}, device_id_type=MESH
        )
    for k in range(1, shards):
        pl.semaphore_signal(
            barrier, inc=1, device_id={"dp": lax.rem(dp + k, shards)}, device_id_type=MESH
        )
    pl.semaphore_signal(barrier, inc=1, device_id=other_id, device_id_type=MESH)
    pl.semaphore_wait(barrier, parts - 1 + shards - 1 + 1)

    def remote(src, dst, send, recv, device):
        return pltpu.make_async_remote_copy(
            src_ref=src,
            dst_ref=dst,
            send_sem=send,
            recv_sem=recv,
            device_id=device,
            device_id_type=MESH,
        )

    def owners(q, side):
        return lax.rem(1 + side + q // chunks, 2)

    def token_rows(q, side):
        return tokens_hbm.at[pl.ds(2 * owners(q, side), 2), lax.rem(q, chunks)]

    def columns(s):
        return pl.ds(s * depth, depth)

    def own_copy(q):
        return pltpu.make_async_copy(
            token_rows(q, side), tok.at[q, :, :, columns(0)], own_sem.at[q]
        )

    def sib_copy(q):
        return remote(
            token_rows(q, side), tok.at[q, :, :, columns(1)], sib_send.at[q], sib_recv.at[q], sib_id
        )

    def far_copy(q):
        return remote(
            token_rows(q, 1 - side),
            tok.at[q, :, :, columns(2)],
            far_send.at[q],
            far_recv.at[q],
            far_id,
        )

    def diag_copy(q):
        return remote(
            tok.at[q, :, :, columns(2)],
            tok.at[q, :, :, columns(3)],
            diag_send.at[q],
            diag_recv.at[q],
            sib_id,
        )

    def store_copy(k):
        return remote(
            outbound.at[pl.ds(k * capacity, capacity)],
            inbound.at[pl.ds(k * capacity, capacity)],
            store_send.at[k],
            store_recv.at[k],
            {"dp": lax.rem(dp + k, shards)},
        )

    def back_copy(k):
        return remote(
            outgoing.at[pl.ds(k * capacity, capacity)],
            returned.at[pl.ds(k * capacity, capacity)],
            back_send.at[k],
            back_recv.at[k],
            {"dp": lax.rem(dp + shards - k, shards)},
        )

    def piece_at(g, k):
        return pl.ds(pl.multiple_of((g * share + k) * height, height), height)

    def near(k):
        return lax.rem(low + k, share)

    def piece_copy():
        here = piece_at(group, low)
        return remote(outw.at[0, here], outw.at[2, here], piece_send, piece_recv, far_id)

    def spread_copy(k):
        here = piece_at(group, low)
        return remote(
            outw.at[2, here],
            outw.at[2, here],
            spread_send.at[k],
            spread_recv.at[k],
            {"dp": dp - low + near(k)},
        )

    def across_copy(k):
        here = piece_at(group, near(k))
        return remote(
            outw.at[2, here], outw.at[2, here], across_send.at[k], across_recv.at[k], other_id
        )

    def pass_copy(g, k):
        here = piece_at(g, k)
        n = g * share + k
        return remote(outw.at[2, here], outw.at[3, here], pass_send.at[n], pass_recv.at[n], sib_id)

    def whole_copy():
        n = pieces
        return remote(outw.at[0], outw.at[1], pass_send.at[n], pass_recv.at[n], sib_id)

    def norm_copy(s, j):
        if s == 1:
            t, device = 2 * (chunks + j) + 1 - half, sib_id
        elif s == 2:
            t, device = 2 * j + half, far_id
        else:
            t, device = 2 * j + 1 - half, diag_id
        return remote(
            normed.at[t], got.at[s - 1, j], norm_send.at[s - 1, j], norm_recv.at[s - 1, j], device
        )

    ahead = min(3, rounds)
    for q in range(ahead):
        far_copy(q).start()

    loads[0].wait()
    table_ref[...] = slot_tables(home_ref[...], dp, sessions, shards, capacity)
    table_copy = pltpu.make_async_copy(table_ref, table, table_sem)
    table_copy.start()

    @pl.loop(0, rounds)
    def _(q):
        own_copy(q).start()
        sib_copy(q).start()

    lane = lax.broadcasted_iota(jnp.int32, (slots, slots), 1)
    row = lax.broadcasted_iota(jnp.int32, (slots, slots), 0)
    pair = 2 * head_size
    wide = 256
    tall = lax.broadcasted_iota(jnp.int32, (wide, wide), 0)
    flat = lax.broadcasted_iota(jnp.int32, (wide, wide), 1)
    band = wide // sessions
    swap_in = (flat == lax.rem(tall, band) * sessions + tall // band).astype(BF16)
    swap_out = (flat == lax.rem(tall, sessions) * band + tall // sessions).astype(BF16)
    blocks = store_ref.shape[1] // band

    loads[1].wait()

    @pl.loop(0, blocks)
    def _(b):
        base = b * (band * 128)
        stacked = jnp.concatenate(
            [
                raw_store[:, pl.ds(pl.multiple_of(base + a * 128, 128), 128)]
                for a in range(band)
            ],
            axis=0,
        )
        moved = jnp.dot(swap_in, stacked, preferred_element_type=F32).astype(BF16)
        at = pl.ds(pl.multiple_of(b * band, band), band)
        store_ref[:, at, :] = moved.reshape(sessions, band, 128)

    table_copy.wait()
    for k in range(1, shards):
        for c in range(capacity):
            outbound[k * capacity + c] = store_ref[look(2, k * capacity + c, sessions)]
        store_copy(k).start()
    for c in range(capacity):
        inbound[c] = store_ref[look(2, c, sessions)]

    within = lax.rem(lane, head_size)
    first = within < head_size // 2
    places = row == 2 * within + lane // head_size
    spread = places.astype(BF16)
    back = (lane == 2 * lax.rem(row, head_size) + row // head_size).astype(BF16)
    tile = min(512, model)

    loads[2].wait()

    @pl.loop(0, model // tile)
    def _(t):
        cols = pl.ds(pl.multiple_of(t * tile, tile), tile)
        for g in range(heads // 2):
            part = slice(g * pair, (g + 1) * pair)
            moved = jnp.dot(back, outw[0, part, cols], preferred_element_type=F32)
            outw[0, part, cols] = moved.astype(BF16)

    piece_copy().start()
    whole_copy().start()

    eye = lax.broadcasted_iota(jnp.int32, (heads, heads), 0) == lax.broadcasted_iota(
        jnp.int32, (heads, heads), 1
    )
    rate_col = jnp.sum(jnp.where(eye, rate_ref[...], 0.0), axis=1, keepdims=True)
    bias_col = jnp.sum(jnp.where(eye, bias_ref[...], 0.0), axis=1, keepdims=True)
    causal = row >= lane
    gains = []
    for g in range(heads // 2):
        column = jnp.sum(
            jnp.where(row == lane, gain_ref[:, g * pair : (g + 1) * pair], 0.0),
            axis=1,
            keepdims=True,
        )
        gains.append(jnp.sum(jnp.where(places, column, 0.0), axis=0, keepdims=True))

    for load in loads[3:]:
        load.wait()

    for s in range(parts):
        start = xor_place(me, s) * depth
        for b in range(depth // 128):
            cut = dtw_ref[:, pl.ds(pl.multiple_of(start + b * 128, 128), 128)].astype(F32)
            cut = jnp.concatenate([cut, jnp.zeros((128 - heads, 128), F32)], axis=0)
            at = slice(s * depth + b * 128, s * depth + (b + 1) * 128)
            bd_ref[at, 2 * state_size :] = cut.T.astype(BF16)

    @pl.loop(0, parts)
    def _(t):
        part = pl.ds(pl.multiple_of(t * depth, depth), depth)
        for ref in (x_ref, z_ref):
            for g in range(heads // 2):
                cols = slice(g * pair, (g + 1) * pair)
                moved = jnp.dot(ref[part, cols], spread, preferred_element_type=F32)
                ref[part, cols] = moved.astype(BF16)

    line = lax.broadcasted_iota(jnp.int32, pick_ref.shape, 0)
    spot = lax.broadcasted_iota(jnp.int32, pick_ref.shape, 1)
    fade_spot = spot - heads * 128
    fade_head = 2 * (fade_spot // pair) + jnp.where(
        lax.rem(fade_spot, head_size) < head_size // 2, 0, 1
    )
    for_cum = (spot < heads * 128) & (line < 3 * heads) & (lax.rem(line, heads) == spot // 128)
    for_fade = (spot >= heads * 128) & (line >= 3 * heads) & (line < 5 * heads)
    for_fade = for_fade & (lax.rem(line, heads) == fade_head)
    pick_ref[...] = jnp.where(for_cum | for_fade, 1.0, 0.0).astype(BF16)

    def terms(value, n):
        found = []
        for _ in range(n):
            found.append(value.astype(BF16).astype(F32))
            value = value - found[-1]
        return found

    def prepare(q, raw):
        raw = raw.T[:heads]
        raw = jnp.concatenate([raw[:, :slots] + bias_col, raw[:, slots:] + bias_col], axis=0)
        limits = [
            jnp.full((heads, slots), counts[session_of(q, o)], jnp.int32) for o in range(2)
        ]
        lane8 = lax.broadcasted_iota(jnp.int32, (2 * heads, slots), 1)
        dt_t = jnp.maximum(raw, 0.0) + jnp.log1p(jnp.exp(-jnp.abs(raw)))
        dt_t = jnp.where(lane8 < jnp.concatenate(limits, axis=0), dt_t, 0.0)
        cum_t = dt_t * jnp.concatenate([rate_col, rate_col], axis=0)
        shift = 1
        while shift < slots:
            moved = pltpu.roll(cum_t, shift, axis=1)
            cum_t = cum_t + jnp.where(lane8 >= shift, moved, 0.0)
            shift *= 2
        last = cum_t[:, slots - 1 : slots]
        weigh_t = jnp.exp(cum_t - last) * dt_t
        fade_t = jnp.exp(-cum_t)
        keep_t = jnp.broadcast_to(fade_t[:, slots - 1 : slots], fade_t.shape)
        for o in range(2):
            part = slice(o * heads, (o + 1) * heads)
            rows_ref[2 * q + o] = jnp.concatenate(
                [value[part] for value in (cum_t, dt_t, weigh_t, keep_t)], axis=0
            )
            table_t = terms(cum_t[part], 3) + terms(fade_t[part], 2)
            table_t.append(jnp.zeros((128 - 5 * heads, slots), F32))
            cols_ref[2 * q + o] = jnp.concatenate(table_t, axis=0).T.astype(BF16)

    def session_of(q, o):
        return (2 * owners(q, side) + o) * chunks + lax.rem(q, chunks)

    def session(q, o):
        t = 2 * q + o
        index = session_of(q, o)
        count = counts[index]
        spot = look(0, index, shards * capacity)
        rows_t = rows_ref[t]
        cols_t = cols_ref[t]
        bc = bc_ref[t]
        b_t = bc.astype(F32).T[:state_size]
        c_bf = bc[:, state_size:]
        scores = lax.dot_general(
            c_bf, bc[:, :state_size], (((1,), (1,)), ((), ())), preferred_element_type=F32
        )
        gated_parts = []
        squares = None
        for g in range(heads // 2):
            cols = slice(g * pair, (g + 1) * pair)
            xs = xs_ref[t, :, cols]
            zs = zs_ref[t, :, cols].astype(F32)
            split = jnp.concatenate(
                [jnp.where(first, xs, jnp.zeros((), BF16)), jnp.where(first, jnp.zeros((), BF16), xs)],
                axis=0,
            )
            mixes = []
            weighed = []
            ends = jnp.dot(
                cols_t, pick_ref[:, g * 256 : (g + 1) * 256], preferred_element_type=F32
            )
            for h in (2 * g, 2 * g + 1):
                end = ends[:, (h % 2) * 128 : (h % 2 + 1) * 128]
                gaps = jnp.where(causal, rows_t[h : h + 1] - end, -1e30)
                mixes.append(
                    (jnp.exp(gaps) * rows_t[heads + h : heads + h + 1] * scores).astype(BF16)
                )
                weighed.append((b_t * rows_t[2 * heads + h : 2 * heads + h + 1]).astype(BF16))
            y = jnp.dot(jnp.concatenate(mixes, axis=1), split, preferred_element_type=F32)
            part = slice(g * head_size, (g + 1) * head_size)
            kept = inbound[spot, part, :]
            halves = jnp.concatenate([kept[:, :state_size], kept[:, state_size:]], axis=0)
            carried = lax.dot_general(
                c_bf, halves, (((1,), (1,)), ((), ())), preferred_element_type=F32
            )
            at = heads * 128 + g * pair
            fades = jnp.dot(cols_t, pick_ref[:, at : at + pair], preferred_element_type=F32)
            y = y + carried * fades
            grown = jnp.dot(
                jnp.concatenate(weighed, axis=1), split, preferred_element_type=F32
            ).T
            keep = jnp.where(
                row[:head_size] < head_size // 2,
                rows_t[3 * heads + 2 * g : 3 * heads + 2 * g + 1],
                rows_t[3 * heads + 2 * g + 1 : 3 * heads + 2 * g + 2],
            )
            grown = jnp.concatenate([grown[:head_size], grown[head_size:]], axis=1)
            state_ref[index, part, :] = (keep * kept.astype(F32) + grown).astype(BF16)
            gated = y * (zs * jax.nn.sigmoid(zs))
            square = gated * gated
            squares = square if squares is None else squares + square
            gated_parts.append(gated)
        squares = jnp.sum(squares, axis=1, keepdims=True)
        scale = lax.rsqrt(squares * (1.0 / inner) + 1e-05)
        scale = jnp.where(row[:, :1] < count, scale, 0.0)
        for g in range(heads // 2):
            cols = slice(g * pair, (g + 1) * pair)
            normed[t, :, cols] = (gated_parts[g] * scale * gains[g]).astype(BF16)

    def project(q):
        own_copy(q).wait()
        sib_copy(q).wait_recv()
        diag_copy(q).wait_recv()
        values = tok[q].reshape(rows, parts * depth)
        at = pl.ds(2 * q, 2)
        total = jnp.dot(values, bd_ref[...], preferred_element_type=F32)
        bc_ref[at] = total[:, : 2 * state_size].astype(BF16).reshape(2, slots, 2 * state_size)
        prepare(q, total[:, 2 * state_size :])
        for weight, ref in ((x_ref, xs_ref), (z_ref, zs_ref)):
            total = jnp.dot(values, weight[...], preferred_element_type=F32)
            ref[at] = total.astype(BF16).reshape(2, slots, inner)

    def reached(q):
        return jnp.where(q < lag, 0, jnp.minimum(jnp.minimum(2 * (q - lag + 1), q), rounds))

    def round_trip(q, carry):
        @pl.when(q < rounds)
        def _():
            far_copy(q).wait_recv()
            diag_copy(q).start()

        @pl.when(q + ahead < rounds)
        def _():
            far_copy(q + ahead).start()

        @pl.when(q == 1)
        def _():
            piece_copy().wait_recv()
            across_copy(0).start()
            pass_copy(group, low).start()

        @pl.when(q == lag)
        def _():
            for k in range(1, shards):
                store_copy(k).wait_recv()
            for k in range(1, share):
                spread_copy(k).start()

        @pl.when(q == rounds - 1)
        def _():
            for j in range(chunks):
                norm_copy(2, j).start()
                norm_copy(3, j).start()

        @pl.loop(reached(q - 1), reached(q))
        def _(done):
            session(done, 0)
            session(done, 1)

        @pl.when(q < rounds)
        def _():
            project(q)

        return carry

    lax.fori_loop(0, rounds + 1, round_trip, 0)

    for k in range(1, shards):
        for c in range(capacity):
            outgoing[k * capacity + c] = state_ref[look(3, k * capacity + c, sessions)]
        back_copy(k).start()
    for j in range(chunks):
        norm_copy(1, j).start()
    for k in range(1, share):
        spread_copy(k).wait_recv()
        across_copy(share - k).start()
        pass_copy(group, near(share - k)).start()
    for c in range(capacity):
        returned[c] = state_ref[look(3, c, sessions)]

    whole_copy().wait_recv()
    for j in range(chunks):
        norm_copy(1, j).wait_recv()

    @pl.loop(0, model // tile)
    def _(t):
        cols = pl.ds(pl.multiple_of(t * tile, tile), tile)
        mine = jnp.concatenate([normed[2 * (chunks + j) + half] for j in range(chunks)], axis=0)
        total = jnp.dot(mine, outw[0, :, cols], preferred_element_type=F32)
        theirs = got[0].reshape(chunks * slots, inner)
        total += jnp.dot(theirs, outw[1, :, cols], preferred_element_type=F32)
        sums[:, :, cols] = total.reshape(chunks, slots, tile)

    for k in range(share):
        across_copy(k).wait_recv()
        pass_copy(1 - group, near(k)).start()
    for k in range(share):
        pass_copy(group, near(k)).wait_recv()
        pass_copy(1 - group, near(k)).wait_recv()

    writes = []
    for pos in range(0, chunks, 2):
        for j in (pos, pos + 1):
            norm_copy(2, j).wait_recv()
            norm_copy(3, j).wait_recv()

        @pl.loop(0, model // tile)
        def _(t):
            cols = pl.ds(pl.multiple_of(t * tile, tile), tile)
            total = sums[pos : pos + 2, :, cols].reshape(rows, tile)
            for s in (2, 3):
                total += jnp.dot(
                    got[s - 1, pos : pos + 2].reshape(rows, inner),
                    outw[s, :, cols],
                    preferred_element_type=F32,
                )
            out_ref[pl.ds(pos * slots, rows), cols] = total.astype(BF16)

        there = pl.ds(pos * slots, rows)
        writes.append(pltpu.make_async_copy(out_ref.at[there], out_hbm.at[there], write_sem.at[pos]))
        writes[-1].start()

    for k in range(1, shards):
        back_copy(k).wait_recv()

    @pl.loop(0, blocks)
    def _(b):
        at = pl.ds(pl.multiple_of(b * band, band), band)
        stacked = jnp.concatenate([returned[look(1, r, shards * capacity), at, :] for r in range(sessions)], axis=0)
        moved = jnp.dot(swap_out, stacked, preferred_element_type=F32).astype(BF16)
        base = b * (band * 128)
        for a in range(band):
            raw_store[:, pl.ds(pl.multiple_of(base + a * 128, 128), 128)] = moved[
                a * sessions : (a + 1) * sessions
            ]

    writes.append(pltpu.make_async_copy(raw_store, new_store_hbm, write_sem.at[chunks]))
    writes[-1].start()

    @pl.loop(0, rounds)
    def _(q):
        far_copy(q).wait_send()
        sib_copy(q).wait_send()
        diag_copy(q).wait_send()

    for j in range(chunks):
        for s in range(1, parts):
            norm_copy(s, j).wait_send()
    for k in range(1, shards):
        store_copy(k).wait_send()
        back_copy(k).wait_send()
    piece_copy().wait_send()
    whole_copy().wait_send()
    for k in range(share):
        if k:
            spread_copy(k).wait_send()
        across_copy(k).wait_send()
        pass_copy(0, k).wait_send()
        pass_copy(1, k).wait_send()
    for write in writes:
        write.wait()


def run_layer(counts, home, tokens4, store, weights, params, out_weight, sizes, shards, capacity):
    heads, head_size, state_size = sizes
    parts, chunks, slots, depth = tokens4.shape
    x_weight, z_weight, bc_weight, dt_weight = weights
    inner = heads * head_size
    model = out_weight.shape[1]
    sessions, state_width = store.shape
    share = min(4, shards)
    pieces = 2 * share
    rounds = 2 * chunks
    vmem = pl.BlockSpec(memory_space=pltpu.VMEM)
    hbm = pl.BlockSpec(memory_space=pl.ANY)
    dma = pltpu.SemaphoreType.DMA
    state = (state_width // 128, 128)
    exchange = pltpu.VMEM((shards * capacity,) + state, BF16)
    kept = pltpu.VMEM((sessions,) + state, BF16)
    width = parts * depth
    return pl.pallas_call(
        functools.partial(
            layer_kernel, heads, head_size, state_size, chunks, parts, shards, share, capacity
        ),
        out_shape=(
            jax.ShapeDtypeStruct((chunks * slots, model), BF16),
            jax.ShapeDtypeStruct(store.shape, BF16),
        ),
        in_specs=[pl.BlockSpec(memory_space=pltpu.SMEM)] + [hbm] * 6 + [vmem] * 4 + [hbm],
        out_specs=(hbm, hbm),
        scratch_shapes=[
            pltpu.VMEM((width, inner), BF16),
            pltpu.VMEM((width, inner), BF16),
            pltpu.VMEM((width, 2 * state_size + 128), BF16),
            pltpu.VMEM((parts, inner, model), BF16),
            pltpu.VMEM((rounds, 2, slots, width), BF16),
            pltpu.VMEM(home.shape, jnp.int32),
            pltpu.VMEM((8, 128), jnp.int32),
            pltpu.SMEM((8, 128), jnp.int32),
            pltpu.VMEM(store.shape, BF16),
            kept,
            exchange,
            exchange,
            kept,
            exchange,
            exchange,
            pltpu.VMEM((sessions, slots, inner), BF16),
            pltpu.VMEM((sessions, slots, inner), BF16),
            pltpu.VMEM((sessions, slots, 2 * state_size), BF16),
            pltpu.VMEM((sessions, 4 * heads, slots), F32),
            pltpu.VMEM((sessions, slots, 128), BF16),
            pltpu.VMEM((128, heads * 128 + inner), BF16),
            pltpu.VMEM((sessions, slots, inner), BF16),
            pltpu.VMEM((parts - 1, chunks, slots, inner), BF16),
            pltpu.VMEM((chunks, slots, model), F32),
            pltpu.VMEM((chunks * slots, model), BF16),
            dma((3 + 3 * parts,)),
            dma,
        ]
        + [dma((rounds,))] * 7
        + [dma((shards,))] * 4
        + [dma, dma]
        + [dma((share,))] * 4
        + [dma((pieces + 1,))] * 2
        + [dma((parts - 1, chunks))] * 2
        + [dma((chunks + 1,))],
        compiler_params=pltpu.CompilerParams(
            vmem_limit_bytes=62 * 1024 * 1024, collective_id=0, has_side_effects=True
        ),
        cost_estimate=pl.CostEstimate(
            flops=2 * sessions * slots * width * (2 * inner + 256 + model // parts),
            bytes_accessed=16 * 1024 * 1024,
            transcendentals=sessions * slots * heads * slots,
        ),
        name="layer",
    )(
        counts,
        home,
        tokens4,
        store,
        x_weight,
        z_weight,
        bc_weight,
        dt_weight.T,
        *params,
        out_weight,
    )


def body(
    tokens,
    x_weight,
    z_weight,
    bc_weight,
    dt_weight,
    dt_bias,
    decay_rate,
    norm_gain,
    out_weight,
    store_states,
    home_rows,
    event_counts,
):
    shards = lax.axis_size("dp")
    parts = lax.axis_size("mp")
    sessions = store_states.shape[0]
    capacity = max(2, (sessions + shards - 1) // shards)
    heads = dt_bias.shape[0]
    inner = x_weight.shape[1]
    state_size = bc_weight.shape[1] // 2
    slots = tokens.shape[0] // sessions
    tokens4 = tokens.reshape(parts, sessions // parts, slots, tokens.shape[1])
    return run_layer(
        event_counts,
        home_rows[None, :],
        tokens4,
        store_states,
        (x_weight, z_weight, bc_weight, dt_weight),
        (dt_bias[None, :], decay_rate[None, :], norm_gain[None, :]),
        out_weight,
        (heads, inner // heads, state_size),
        shards,
        capacity,
    )


def solution(mesh):
    return jax.shard_map(
        body,
        mesh=mesh,
        in_specs=(
            P(("groups", "dp"), "mp"),
            P(None, "mp"),
            P(None, "mp"),
            P(None, "mp"),
            P(None, "mp"),
            P("mp"),
            P("mp"),
            P("mp"),
            P("mp", None),
            P(("groups", "dp"), "mp"),
            P("groups"),
            P(("groups", "dp")),
        ),
        out_specs=(P(("groups", "dp", "mp"), None), P(("groups", "dp"), "mp")),
        check_vma=False,
    )
```

```python
import functools

import jax
import jax.numpy as jnp
from jax import lax
from jax.experimental import pallas as pl
from jax.experimental.pallas import tpu as pltpu
from jax.sharding import PartitionSpec as P

F32 = jnp.float32
BF16 = jnp.bfloat16
MESH = pl.DeviceIdType.MESH


def xor_place(me, mask):
    return lax.rem(lax.rem(me, 2) + mask % 2, 2) + 2 * lax.rem(me // 2 + mask // 2, 2)


def wrap(value, size):
    return jnp.where(value >= size, value - size, value)


def slot_tables(home, dp, sessions, shards, capacity):
    total = home.shape[1]
    base = (dp * sessions).astype(F32)
    here = dp.astype(F32)
    home = home.astype(F32)
    who = lax.broadcasted_iota(jnp.int32, (sessions, total), 1).astype(F32)
    spot = lax.broadcasted_iota(jnp.int32, (sessions, total), 0).astype(F32) + base
    owner = jnp.sum(jnp.where(home == spot, who, 0.0), axis=1, keepdims=True)
    wanted = jnp.sum(jnp.where(who == spot, home, 0.0), axis=1, keepdims=True)
    server = jnp.floor(owner * (1.0 / sessions))
    shard = jnp.floor(wanted * (1.0 / sessions))
    place = lax.broadcasted_iota(jnp.int32, (sessions, 128), 0).astype(F32)
    lane = lax.broadcasted_iota(jnp.int32, (sessions, 128), 1).astype(F32)

    def as_row(column):
        return jnp.sum(jnp.where(place == lane, column, 0.0), axis=0, keepdims=True)

    def rank(keys, order):
        earlier = (as_row(keys) == keys) & (as_row(order) < order) & (lane < sessions)
        return jnp.sum(jnp.where(earlier, 1.0, 0.0), axis=1, keepdims=True)

    to_server = wrap(server - here + shards, shards)
    from_home = wrap(here - shard + shards, shards)
    row_slot = to_server * capacity + rank(server, place[:, :1])
    session_slot = from_home * capacity + rank(shard, wanted - shard * sessions)

    def holder(slots):
        return jnp.sum(jnp.where(slots == lane, place, 0.0), axis=0, keepdims=True)

    rows = [as_row(session_slot), as_row(row_slot), holder(row_slot), holder(session_slot)]
    return jnp.concatenate(rows + [jnp.zeros((4, 128), F32)], axis=0).astype(jnp.int32)


def layer_kernel(
    heads,
    head_size,
    state_size,
    chunks,
    parts,
    shards,
    share,
    capacity,
    counts,
    home_hbm,
    tokens_hbm,
    store_hbm,
    x_hbm,
    z_hbm,
    bc_hbm,
    dtw_ref,
    bias_ref,
    rate_ref,
    gain_ref,
    outw_hbm,
    out_ref,
    new_store_ref,
    x_ref,
    z_ref,
    bd_ref,
    outw,
    tok,
    home_ref,
    table_ref,
    table,
    raw_store,
    store_ref,
    outbound,
    inbound,
    state_ref,
    outgoing,
    upper,
    lower,
    xs_ref,
    zs_ref,
    bc_ref,
    rows_ref,
    cols_ref,
    pick_ref,
    normed,
    got,
    sums,
    load_sem,
    table_sem,
    own_sem,
    sib_send,
    sib_recv,
    far_send,
    far_recv,
    diag_send,
    diag_recv,
    store_send,
    store_recv,
    back_send,
    back_recv,
    piece_send,
    piece_recv,
    spread_send,
    spread_recv,
    across_send,
    across_recv,
    pass_send,
    pass_recv,
    norm_send,
    norm_recv,
):
    slots = tokens_hbm.shape[2]
    depth = tokens_hbm.shape[3]
    model = outw_hbm.shape[1]
    inner = heads * head_size
    sessions = chunks * parts
    rounds = 2 * chunks
    lag = rounds // 2
    rows = 2 * slots
    me = lax.axis_index("mp")
    dp = lax.axis_index("dp")
    group = lax.axis_index("groups")
    half = lax.rem(me, 2)
    side = me // 2
    low = lax.rem(dp, share)
    pieces = 2 * share
    height = inner // pieces
    sib_id = {"mp": xor_place(me, 1)}
    far_id = {"mp": xor_place(me, 2)}
    diag_id = {"mp": xor_place(me, 3)}
    tail = state_ref.shape[1] // 2
    returned = (upper, lower)
    other_id = {"groups": 1 - group}

    def look(line, at, size):
        return jnp.minimum(jnp.maximum(table[line, at], 0), size - 1)

    loads = [
        pltpu.make_async_copy(home_hbm, home_ref, load_sem.at[0]),
        pltpu.make_async_copy(store_hbm, raw_store, load_sem.at[1]),
        pltpu.make_async_copy(outw_hbm, outw.at[0], load_sem.at[2]),
    ]
    for s in range(parts):
        part = pl.ds(pl.multiple_of(xor_place(me, s) * depth, depth), depth)
        there = pl.ds(s * depth, depth)
        loads.append(pltpu.make_async_copy(x_hbm.at[part], x_ref.at[there], load_sem.at[3 + 3 * s]))
        loads.append(pltpu.make_async_copy(z_hbm.at[part], z_ref.at[there], load_sem.at[4 + 3 * s]))
        loads.append(
            pltpu.make_async_copy(
                bc_hbm.at[part], bd_ref.at[there, pl.ds(0, 2 * state_size)], load_sem.at[5 + 3 * s]
            )
        )
    for load in loads:
        load.start()

    barrier = pltpu.get_barrier_semaphore()
    for mask in range(1, parts):
        pl.semaphore_signal(
            barrier, inc=1, device_id={"mp": xor_place(me, mask)}, device_id_type=MESH
        )
    for k in range(1, shards):
        pl.semaphore_signal(
            barrier, inc=1, device_id={"dp": lax.rem(dp + k, shards)}, device_id_type=MESH
        )
    pl.semaphore_signal(barrier, inc=1, device_id=other_id, device_id_type=MESH)
    pl.semaphore_wait(barrier, parts - 1 + shards - 1 + 1)

    def remote(src, dst, send, recv, device):
        return pltpu.make_async_remote_copy(
            src_ref=src,
            dst_ref=dst,
            send_sem=send,
            recv_sem=recv,
            device_id=device,
            device_id_type=MESH,
        )

    def owners(q, side):
        return lax.rem(1 + side + q // chunks, 2)

    def token_rows(q, side):
        return tokens_hbm.at[pl.ds(2 * owners(q, side), 2), lax.rem(q, chunks)]

    def columns(s):
        return pl.ds(s * depth, depth)

    def own_copy(q):
        return pltpu.make_async_copy(
            token_rows(q, side), tok.at[q, :, :, columns(0)], own_sem.at[q]
        )

    def sib_copy(q):
        return remote(
            token_rows(q, side), tok.at[q, :, :, columns(1)], sib_send.at[q], sib_recv.at[q], sib_id
        )

    def far_copy(q):
        return remote(
            token_rows(q, 1 - side),
            tok.at[q, :, :, columns(2)],
            far_send.at[q],
            far_recv.at[q],
            far_id,
        )

    def diag_copy(q):
        return remote(
            tok.at[q, :, :, columns(2)],
            tok.at[q, :, :, columns(3)],
            diag_send.at[q],
            diag_recv.at[q],
            sib_id,
        )

    def store_copy(k):
        return remote(
            outbound.at[pl.ds(k * capacity, capacity)],
            inbound.at[pl.ds(k * capacity, capacity)],
            store_send.at[k],
            store_recv.at[k],
            {"dp": lax.rem(dp + k, shards)},
        )

    def back_copy(k, n):
        there = pl.ds(n * tail, tail)
        return remote(
            outgoing.at[pl.ds(k * capacity, capacity), there],
            returned[n].at[pl.ds(k * capacity, capacity)],
            back_send.at[k, n],
            back_recv.at[k, n],
            {"dp": lax.rem(dp + shards - k, shards)},
        )

    def piece_at(g, k):
        return pl.ds(pl.multiple_of((g * share + k) * height, height), height)

    def near(k):
        return lax.rem(low + k, share)

    def piece_copy():
        here = piece_at(group, low)
        return remote(outw.at[0, here], outw.at[2, here], piece_send, piece_recv, far_id)

    def spread_copy(k):
        here = piece_at(group, low)
        return remote(
            outw.at[2, here],
            outw.at[2, here],
            spread_send.at[k],
            spread_recv.at[k],
            {"dp": dp - low + near(k)},
        )

    def across_copy(k):
        here = piece_at(group, near(k))
        return remote(
            outw.at[2, here], outw.at[2, here], across_send.at[k], across_recv.at[k], other_id
        )

    def pass_copy(g, k):
        here = piece_at(g, k)
        n = g * share + k
        return remote(outw.at[2, here], outw.at[3, here], pass_send.at[n], pass_recv.at[n], sib_id)

    def whole_copy():
        n = pieces
        return remote(outw.at[0], outw.at[1], pass_send.at[n], pass_recv.at[n], sib_id)

    def norm_copy(s, j):
        if s == 1:
            t, device = 2 * (chunks + j) + 1 - half, sib_id
        elif s == 2:
            t, device = 2 * j + half, far_id
        else:
            t, device = 2 * j + 1 - half, diag_id
        return remote(
            normed.at[t], got.at[s - 1, j], norm_send.at[s - 1, j], norm_recv.at[s - 1, j], device
        )

    ahead = min(3, rounds)
    for q in range(ahead):
        far_copy(q).start()

    loads[0].wait()
    table_ref[...] = slot_tables(home_ref[...], dp, sessions, shards, capacity)
    table_copy = pltpu.make_async_copy(table_ref, table, table_sem)
    table_copy.start()

    @pl.loop(0, rounds)
    def _(q):
        own_copy(q).start()
        sib_copy(q).start()

    lane = lax.broadcasted_iota(jnp.int32, (slots, slots), 1)
    row = lax.broadcasted_iota(jnp.int32, (slots, slots), 0)
    pair = 2 * head_size
    wide = 256
    tall = lax.broadcasted_iota(jnp.int32, (wide, wide), 0)
    flat = lax.broadcasted_iota(jnp.int32, (wide, wide), 1)
    band = wide // sessions
    swap_in = (flat == lax.rem(tall, band) * sessions + tall // band).astype(BF16)
    swap_out = (flat == lax.rem(tall, sessions) * band + tall // sessions).astype(BF16)
    blocks = store_ref.shape[1] // band

    loads[1].wait()

    @pl.loop(0, blocks)
    def _(b):
        base = b * (band * 128)
        stacked = jnp.concatenate(
            [
                raw_store[:, pl.ds(pl.multiple_of(base + a * 128, 128), 128)]
                for a in range(band)
            ],
            axis=0,
        )
        moved = jnp.dot(swap_in, stacked, preferred_element_type=F32).astype(BF16)
        at = pl.ds(pl.multiple_of(b * band, band), band)
        store_ref[:, at, :] = moved.reshape(sessions, band, 128)

    table_copy.wait()
    for k in range(1, shards):
        for c in range(capacity):
            outbound[k * capacity + c] = store_ref[look(2, k * capacity + c, sessions)]
        store_copy(k).start()
    for c in range(capacity):
        inbound[c] = store_ref[look(2, c, sessions)]

    within = lax.rem(lane, head_size)
    first = within < head_size // 2
    places = row == 2 * within + lane // head_size
    spread = places.astype(BF16)
    back = (lane == 2 * lax.rem(row, head_size) + row // head_size).astype(BF16)
    tile = min(512, model)

    loads[2].wait()

    @pl.loop(0, model // tile)
    def _(t):
        cols = pl.ds(pl.multiple_of(t * tile, tile), tile)
        for g in range(heads // 2):
            part = slice(g * pair, (g + 1) * pair)
            moved = jnp.dot(back, outw[0, part, cols], preferred_element_type=F32)
            outw[0, part, cols] = moved.astype(BF16)

    piece_copy().start()
    whole_copy().start()

    eye = lax.broadcasted_iota(jnp.int32, (heads, heads), 0) == lax.broadcasted_iota(
        jnp.int32, (heads, heads), 1
    )
    rate_col = jnp.sum(jnp.where(eye, rate_ref[...], 0.0), axis=1, keepdims=True)
    bias_col = jnp.sum(jnp.where(eye, bias_ref[...], 0.0), axis=1, keepdims=True)
    causal = row >= lane
    gains = []
    for g in range(heads // 2):
        column = jnp.sum(
            jnp.where(row == lane, gain_ref[:, g * pair : (g + 1) * pair], 0.0),
            axis=1,
            keepdims=True,
        )
        gains.append(jnp.sum(jnp.where(places, column, 0.0), axis=0, keepdims=True))

    for load in loads[3:]:
        load.wait()

    for s in range(parts):
        start = xor_place(me, s) * depth
        for b in range(depth // 128):
            cut = dtw_ref[:, pl.ds(pl.multiple_of(start + b * 128, 128), 128)].astype(F32)
            cut = jnp.concatenate([cut, jnp.zeros((128 - heads, 128), F32)], axis=0)
            at = slice(s * depth + b * 128, s * depth + (b + 1) * 128)
            bd_ref[at, 2 * state_size :] = cut.T.astype(BF16)

    @pl.loop(0, parts)
    def _(t):
        part = pl.ds(pl.multiple_of(t * depth, depth), depth)
        for ref in (x_ref, z_ref):
            for g in range(heads // 2):
                cols = slice(g * pair, (g + 1) * pair)
                moved = jnp.dot(ref[part, cols], spread, preferred_element_type=F32)
                ref[part, cols] = moved.astype(BF16)

    line = lax.broadcasted_iota(jnp.int32, pick_ref.shape, 0)
    spot = lax.broadcasted_iota(jnp.int32, pick_ref.shape, 1)
    fade_spot = spot - heads * 128
    fade_head = 2 * (fade_spot // pair) + jnp.where(
        lax.rem(fade_spot, head_size) < head_size // 2, 0, 1
    )
    for_cum = (spot < heads * 128) & (line < 3 * heads) & (lax.rem(line, heads) == spot // 128)
    for_fade = (spot >= heads * 128) & (line >= 3 * heads) & (line < 5 * heads)
    for_fade = for_fade & (lax.rem(line, heads) == fade_head)
    pick_ref[...] = jnp.where(for_cum | for_fade, 1.0, 0.0).astype(BF16)

    def terms(value, n):
        found = []
        for _ in range(n):
            found.append(value.astype(BF16).astype(F32))
            value = value - found[-1]
        return found

    def prepare(q, raw):
        raw = raw.T[:heads]
        raw = jnp.concatenate([raw[:, :slots] + bias_col, raw[:, slots:] + bias_col], axis=0)
        limits = [
            jnp.full((heads, slots), counts[session_of(q, o)], jnp.int32) for o in range(2)
        ]
        lane8 = lax.broadcasted_iota(jnp.int32, (2 * heads, slots), 1)
        dt_t = jnp.maximum(raw, 0.0) + jnp.log1p(jnp.exp(-jnp.abs(raw)))
        dt_t = jnp.where(lane8 < jnp.concatenate(limits, axis=0), dt_t, 0.0)
        cum_t = dt_t * jnp.concatenate([rate_col, rate_col], axis=0)
        shift = 1
        while shift < slots:
            moved = pltpu.roll(cum_t, shift, axis=1)
            cum_t = cum_t + jnp.where(lane8 >= shift, moved, 0.0)
            shift *= 2
        last = cum_t[:, slots - 1 : slots]
        weigh_t = jnp.exp(cum_t - last) * dt_t
        fade_t = jnp.exp(-cum_t)
        keep_t = jnp.broadcast_to(fade_t[:, slots - 1 : slots], fade_t.shape)
        for o in range(2):
            part = slice(o * heads, (o + 1) * heads)
            rows_ref[2 * q + o] = jnp.concatenate(
                [value[part] for value in (cum_t, dt_t, weigh_t, keep_t)], axis=0
            )
            table_t = terms(cum_t[part], 3) + terms(fade_t[part], 2)
            table_t.append(jnp.zeros((128 - 5 * heads, slots), F32))
            cols_ref[2 * q + o] = jnp.concatenate(table_t, axis=0).T.astype(BF16)

    def session_of(q, o):
        return (2 * owners(q, side) + o) * chunks + lax.rem(q, chunks)

    def session(q, o):
        t = 2 * q + o
        index = session_of(q, o)
        count = counts[index]
        spot = look(0, index, shards * capacity)
        rows_t = rows_ref[t]
        cols_t = cols_ref[t]
        bc = bc_ref[t]
        b_t = bc.astype(F32).T[:state_size]
        c_bf = bc[:, state_size:]
        scores = lax.dot_general(
            c_bf, bc[:, :state_size], (((1,), (1,)), ((), ())), preferred_element_type=F32
        )
        gated_parts = []
        squares = None
        for g in range(heads // 2):
            cols = slice(g * pair, (g + 1) * pair)
            xs = xs_ref[t, :, cols]
            zs = zs_ref[t, :, cols].astype(F32)
            split = jnp.concatenate(
                [jnp.where(first, xs, jnp.zeros((), BF16)), jnp.where(first, jnp.zeros((), BF16), xs)],
                axis=0,
            )
            mixes = []
            weighed = []
            ends = jnp.dot(
                cols_t, pick_ref[:, g * 256 : (g + 1) * 256], preferred_element_type=F32
            )
            for h in (2 * g, 2 * g + 1):
                end = ends[:, (h % 2) * 128 : (h % 2 + 1) * 128]
                gaps = jnp.where(causal, rows_t[h : h + 1] - end, -1e30)
                mixes.append(
                    (jnp.exp(gaps) * rows_t[heads + h : heads + h + 1] * scores).astype(BF16)
                )
                weighed.append((b_t * rows_t[2 * heads + h : 2 * heads + h + 1]).astype(BF16))
            y = jnp.dot(jnp.concatenate(mixes, axis=1), split, preferred_element_type=F32)
            part = slice(g * head_size, (g + 1) * head_size)
            kept = inbound[spot, part, :]
            halves = jnp.concatenate([kept[:, :state_size], kept[:, state_size:]], axis=0)
            carried = lax.dot_general(
                c_bf, halves, (((1,), (1,)), ((), ())), preferred_element_type=F32
            )
            at = heads * 128 + g * pair
            fades = jnp.dot(cols_t, pick_ref[:, at : at + pair], preferred_element_type=F32)
            y = y + carried * fades
            grown = jnp.dot(
                jnp.concatenate(weighed, axis=1), split, preferred_element_type=F32
            ).T
            keep = jnp.where(
                row[:head_size] < head_size // 2,
                rows_t[3 * heads + 2 * g : 3 * heads + 2 * g + 1],
                rows_t[3 * heads + 2 * g + 1 : 3 * heads + 2 * g + 2],
            )
            grown = jnp.concatenate([grown[:head_size], grown[head_size:]], axis=1)
            state_ref[index, part, :] = (keep * kept.astype(F32) + grown).astype(BF16)
            gated = y * (zs * jax.nn.sigmoid(zs))
            square = gated * gated
            squares = square if squares is None else squares + square
            gated_parts.append(gated)
        squares = jnp.sum(squares, axis=1, keepdims=True)
        scale = lax.rsqrt(squares * (1.0 / inner) + 1e-05)
        scale = jnp.where(row[:, :1] < count, scale, 0.0)
        for g in range(heads // 2):
            cols = slice(g * pair, (g + 1) * pair)
            normed[t, :, cols] = (gated_parts[g] * scale * gains[g]).astype(BF16)

    def project(q):
        own_copy(q).wait()
        sib_copy(q).wait_recv()
        diag_copy(q).wait_recv()
        values = tok[q].reshape(rows, parts * depth)
        at = pl.ds(2 * q, 2)
        total = jnp.dot(values, bd_ref[...], preferred_element_type=F32)
        bc_ref[at] = total[:, : 2 * state_size].astype(BF16).reshape(2, slots, 2 * state_size)
        prepare(q, total[:, 2 * state_size :])
        for weight, ref in ((x_ref, xs_ref), (z_ref, zs_ref)):
            total = jnp.dot(values, weight[...], preferred_element_type=F32)
            ref[at] = total.astype(BF16).reshape(2, slots, inner)

    def reached(q):
        return jnp.where(q < lag, 0, jnp.minimum(jnp.minimum(2 * (q - lag + 1), q), rounds))

    def round_trip(q, carry):
        @pl.when(q < rounds)
        def _():
            far_copy(q).wait_recv()
            diag_copy(q).start()

        @pl.when(q + ahead < rounds)
        def _():
            far_copy(q + ahead).start()

        @pl.when(q == 1)
        def _():
            piece_copy().wait_recv()
            across_copy(0).start()
            pass_copy(group, low).start()

        @pl.when(q == lag)
        def _():
            for k in range(1, shards):
                store_copy(k).wait_recv()

        @pl.when(q == lag - 2)
        def _():
            for k in range(1, share):
                spread_copy(k).start()

        @pl.when(q == rounds - 1)
        def _():
            for j in range(chunks):
                norm_copy(2, j).start()
                norm_copy(3, j).start()
            for k in range(1, share):
                spread_copy(k).wait_recv()
                across_copy(share - k).start()
                pass_copy(group, near(share - k)).start()

        @pl.loop(reached(q - 1), reached(q))
        def _(done):
            session(done, 0)
            session(done, 1)

        @pl.when(q < rounds)
        def _():
            project(q)

        return carry

    lax.fori_loop(0, rounds + 1, round_trip, 0)

    for k in range(1, shards):
        for c in range(capacity):
            outgoing[k * capacity + c] = state_ref[look(3, k * capacity + c, sessions)]
    for n in range(2):
        for k in range(1, shards):
            back_copy(k, n).start()
    for j in range(chunks):
        norm_copy(1, j).start()
    for c in range(capacity):
        for n in range(2):
            there = slice(n * tail, (n + 1) * tail)
            returned[n][c] = state_ref[look(3, c, sessions), there, :]

    whole_copy().wait_recv()
    for j in range(chunks):
        norm_copy(1, j).wait_recv()

    @pl.loop(0, model // tile)
    def _(t):
        cols = pl.ds(pl.multiple_of(t * tile, tile), tile)
        mine = jnp.concatenate([normed[2 * (chunks + j) + half] for j in range(chunks)], axis=0)
        total = jnp.dot(mine, outw[0, :, cols], preferred_element_type=F32)
        theirs = got[0].reshape(chunks * slots, inner)
        total += jnp.dot(theirs, outw[1, :, cols], preferred_element_type=F32)
        sums[:, :, cols] = total.reshape(chunks, slots, tile)

    for k in range(share):
        across_copy(k).wait_recv()
        pass_copy(1 - group, near(k)).start()
    for k in range(share):
        pass_copy(group, near(k)).wait_recv()
        pass_copy(1 - group, near(k)).wait_recv()

    for pos in range(0, chunks, 2):
        for j in (pos, pos + 1):
            norm_copy(2, j).wait_recv()
            norm_copy(3, j).wait_recv()

        @pl.loop(0, model // tile)
        def _(t):
            cols = pl.ds(pl.multiple_of(t * tile, tile), tile)
            total = sums[pos : pos + 2, :, cols].reshape(rows, tile)
            for s in (2, 3):
                total += jnp.dot(
                    got[s - 1, pos : pos + 2].reshape(rows, inner),
                    outw[s, :, cols],
                    preferred_element_type=F32,
                )
            out_ref[pl.ds(pos * slots, rows), cols] = total.astype(BF16)

    for n in range(2):
        for k in range(1, shards):
            back_copy(k, n).wait_recv()

        @pl.loop(0, blocks // 2)
        def _(b):
            at = pl.ds(pl.multiple_of(b * band, band), band)
            found = [returned[n][look(1, r, shards * capacity), at, :] for r in range(sessions)]
            moved = jnp.dot(swap_out, jnp.concatenate(found, axis=0), preferred_element_type=F32)
            moved = moved.astype(BF16)
            base = (n * (blocks // 2) + b) * (band * 128)
            for a in range(band):
                new_store_ref[:, pl.ds(pl.multiple_of(base + a * 128, 128), 128)] = moved[
                    a * sessions : (a + 1) * sessions
                ]

    @pl.loop(0, rounds)
    def _(q):
        far_copy(q).wait_send()
        sib_copy(q).wait_send()
        diag_copy(q).wait_send()

    for j in range(chunks):
        for s in range(1, parts):
            norm_copy(s, j).wait_send()
    for k in range(1, shards):
        store_copy(k).wait_send()
        for n in range(2):
            back_copy(k, n).wait_send()
    piece_copy().wait_send()
    whole_copy().wait_send()
    for k in range(share):
        if k:
            spread_copy(k).wait_send()
        across_copy(k).wait_send()
        pass_copy(0, k).wait_send()
        pass_copy(1, k).wait_send()


def run_layer(counts, home, tokens4, store, weights, params, out_weight, sizes, shards, capacity):
    heads, head_size, state_size = sizes
    parts, chunks, slots, depth = tokens4.shape
    x_weight, z_weight, bc_weight, dt_weight = weights
    inner = heads * head_size
    model = out_weight.shape[1]
    sessions, state_width = store.shape
    share = min(4, shards)
    pieces = 2 * share
    rounds = 2 * chunks
    vmem = pl.BlockSpec(memory_space=pltpu.VMEM)
    hbm = pl.BlockSpec(memory_space=pl.ANY)
    dma = pltpu.SemaphoreType.DMA
    state = (state_width // 128, 128)
    exchange = pltpu.VMEM((shards * capacity,) + state, BF16)
    piece = pltpu.VMEM((shards * capacity, state[0] // 2, state[1]), BF16)
    kept = pltpu.VMEM((sessions,) + state, BF16)
    width = parts * depth
    return pl.pallas_call(
        functools.partial(
            layer_kernel, heads, head_size, state_size, chunks, parts, shards, share, capacity
        ),
        out_shape=(
            pltpu.VMEM((chunks * slots, model), BF16),
            pltpu.VMEM(store.shape, BF16),
        ),
        in_specs=[pl.BlockSpec(memory_space=pltpu.SMEM)] + [hbm] * 6 + [vmem] * 4 + [hbm],
        out_specs=(vmem, vmem),
        scratch_shapes=[
            pltpu.VMEM((width, inner), BF16),
            pltpu.VMEM((width, inner), BF16),
            pltpu.VMEM((width, 2 * state_size + 128), BF16),
            pltpu.VMEM((parts, inner, model), BF16),
            pltpu.VMEM((rounds, 2, slots, width), BF16),
            pltpu.VMEM(home.shape, jnp.int32),
            pltpu.VMEM((8, 128), jnp.int32),
            pltpu.SMEM((8, 128), jnp.int32),
            pltpu.VMEM(store.shape, BF16),
            kept,
            exchange,
            exchange,
            kept,
            exchange,
            piece,
            piece,
            pltpu.VMEM((sessions, slots, inner), BF16),
            pltpu.VMEM((sessions, slots, inner), BF16),
            pltpu.VMEM((sessions, slots, 2 * state_size), BF16),
            pltpu.VMEM((sessions, 4 * heads, slots), F32),
            pltpu.VMEM((sessions, slots, 128), BF16),
            pltpu.VMEM((128, heads * 128 + inner), BF16),
            pltpu.VMEM((sessions, slots, inner), BF16),
            pltpu.VMEM((parts - 1, chunks, slots, inner), BF16),
            pltpu.VMEM((chunks, slots, model), F32),
            dma((3 + 3 * parts,)),
            dma,
        ]
        + [dma((rounds,))] * 7
        + [dma((shards,))] * 2
        + [dma((shards, 2))] * 2
        + [dma, dma]
        + [dma((share,))] * 4
        + [dma((pieces + 1,))] * 2
        + [dma((parts - 1, chunks))] * 2,
        compiler_params=pltpu.CompilerParams(
            vmem_limit_bytes=56 * 1024 * 1024, collective_id=0, has_side_effects=True
        ),
        cost_estimate=pl.CostEstimate(
            flops=2 * sessions * slots * width * (2 * inner + 256 + model // parts),
            bytes_accessed=16 * 1024 * 1024,
            transcendentals=sessions * slots * heads * slots,
        ),
        name="layer",
    )(
        counts,
        home,
        tokens4,
        store,
        x_weight,
        z_weight,
        bc_weight,
        dt_weight.T,
        *params,
        out_weight,
    )


def body(
    tokens,
    x_weight,
    z_weight,
    bc_weight,
    dt_weight,
    dt_bias,
    decay_rate,
    norm_gain,
    out_weight,
    store_states,
    home_rows,
    event_counts,
):
    shards = lax.axis_size("dp")
    parts = lax.axis_size("mp")
    sessions = store_states.shape[0]
    capacity = max(2, (sessions + shards - 1) // shards)
    heads = dt_bias.shape[0]
    inner = x_weight.shape[1]
    state_size = bc_weight.shape[1] // 2
    slots = tokens.shape[0] // sessions
    tokens4 = tokens.reshape(parts, sessions // parts, slots, tokens.shape[1])
    return run_layer(
        event_counts,
        home_rows[None, :],
        tokens4,
        store_states,
        (x_weight, z_weight, bc_weight, dt_weight),
        (dt_bias[None, :], decay_rate[None, :], norm_gain[None, :]),
        out_weight,
        (heads, inner // heads, state_size),
        shards,
        capacity,
    )


def solution(mesh):
    return jax.shard_map(
        body,
        mesh=mesh,
        in_specs=(
            P(("groups", "dp"), "mp"),
            P(None, "mp"),
            P(None, "mp"),
            P(None, "mp"),
            P(None, "mp"),
            P("mp"),
            P("mp"),
            P("mp"),
            P("mp", None),
            P(("groups", "dp"), "mp"),
            P("groups"),
            P(("groups", "dp")),
        ),
        out_specs=(P(("groups", "dp", "mp"), None), P(("groups", "dp"), "mp")),
        check_vma=False,
    )
```

```python
import functools

import jax
import jax.numpy as jnp
from jax import lax
from jax.experimental import pallas as pl
from jax.experimental.pallas import tpu as pltpu
from jax.sharding import PartitionSpec as P

F32 = jnp.float32
BF16 = jnp.bfloat16
MESH = pl.DeviceIdType.MESH


def xor_place(me, mask):
    return lax.rem(lax.rem(me, 2) + mask % 2, 2) + 2 * lax.rem(me // 2 + mask // 2, 2)


def wrap(value, size):
    return jnp.where(value >= size, value - size, value)


def slot_tables(home, dp, sessions, shards, capacity):
    total = home.shape[1]
    base = (dp * sessions).astype(F32)
    here = dp.astype(F32)
    home = home.astype(F32)
    who = lax.broadcasted_iota(jnp.int32, (sessions, total), 1).astype(F32)
    spot = lax.broadcasted_iota(jnp.int32, (sessions, total), 0).astype(F32) + base
    owner = jnp.sum(jnp.where(home == spot, who, 0.0), axis=1, keepdims=True)
    wanted = jnp.sum(jnp.where(who == spot, home, 0.0), axis=1, keepdims=True)
    server = jnp.floor(owner * (1.0 / sessions))
    shard = jnp.floor(wanted * (1.0 / sessions))
    place = lax.broadcasted_iota(jnp.int32, (sessions, 128), 0).astype(F32)
    lane = lax.broadcasted_iota(jnp.int32, (sessions, 128), 1).astype(F32)

    def as_row(column):
        return jnp.sum(jnp.where(place == lane, column, 0.0), axis=0, keepdims=True)

    def rank(keys, order):
        earlier = (as_row(keys) == keys) & (as_row(order) < order) & (lane < sessions)
        return jnp.sum(jnp.where(earlier, 1.0, 0.0), axis=1, keepdims=True)

    to_server = wrap(server - here + shards, shards)
    from_home = wrap(here - shard + shards, shards)
    row_slot = to_server * capacity + rank(server, place[:, :1])
    session_slot = from_home * capacity + rank(shard, wanted - shard * sessions)

    def holder(slots):
        return jnp.sum(jnp.where(slots == lane, place, 0.0), axis=0, keepdims=True)

    rows = [as_row(session_slot), as_row(row_slot), holder(row_slot), holder(session_slot)]
    return jnp.concatenate(rows + [jnp.zeros((4, 128), F32)], axis=0).astype(jnp.int32)


def layer_kernel(
    heads,
    head_size,
    state_size,
    chunks,
    parts,
    shards,
    share,
    capacity,
    counts,
    home_hbm,
    tokens_hbm,
    store_hbm,
    x_hbm,
    z_hbm,
    bc_hbm,
    dtw_ref,
    bias_ref,
    rate_ref,
    gain_ref,
    outw_hbm,
    out_ref,
    new_store_ref,
    x_ref,
    z_ref,
    bd_ref,
    outw,
    tok,
    home_ref,
    table_ref,
    table,
    raw_store,
    store_ref,
    outbound,
    inbound,
    state_ref,
    outgoing,
    upper,
    lower,
    xs_ref,
    zs_ref,
    bc_ref,
    rows_ref,
    cols_ref,
    pick_ref,
    normed,
    got,
    sums,
    load_sem,
    table_sem,
    own_sem,
    sib_send,
    sib_recv,
    far_send,
    far_recv,
    diag_send,
    diag_recv,
    store_send,
    store_recv,
    back_send,
    back_recv,
    piece_send,
    piece_recv,
    relay_send,
    relay_recv,
    across_send,
    across_recv,
    pass_send,
    pass_recv,
    norm_send,
    norm_recv,
):
    slots = tokens_hbm.shape[2]
    depth = tokens_hbm.shape[3]
    model = outw_hbm.shape[1]
    inner = heads * head_size
    sessions = chunks * parts
    rounds = 2 * chunks
    lag = max(1, rounds // 2 - 1)
    rows = 2 * slots
    me = lax.axis_index("mp")
    dp = lax.axis_index("dp")
    group = lax.axis_index("groups")
    half = lax.rem(me, 2)
    side = me // 2
    low = lax.rem(dp, share)
    pieces = 2 * share
    height = inner // pieces
    sib_id = {"mp": xor_place(me, 1)}
    far_id = {"mp": xor_place(me, 2)}
    diag_id = {"mp": xor_place(me, 3)}
    tail = state_ref.shape[1] // 2
    returned = (upper, lower)
    other_id = {"groups": 1 - group}

    def look(line, at, size):
        return jnp.minimum(jnp.maximum(table[line, at], 0), size - 1)

    loads = [
        pltpu.make_async_copy(home_hbm, home_ref, load_sem.at[0]),
        pltpu.make_async_copy(store_hbm, raw_store, load_sem.at[1]),
        pltpu.make_async_copy(outw_hbm, outw.at[0], load_sem.at[2]),
    ]
    for s in range(parts):
        part = pl.ds(pl.multiple_of(xor_place(me, s) * depth, depth), depth)
        there = pl.ds(s * depth, depth)
        loads.append(pltpu.make_async_copy(x_hbm.at[part], x_ref.at[there], load_sem.at[3 + 3 * s]))
        loads.append(pltpu.make_async_copy(z_hbm.at[part], z_ref.at[there], load_sem.at[4 + 3 * s]))
        loads.append(
            pltpu.make_async_copy(
                bc_hbm.at[part], bd_ref.at[there, pl.ds(0, 2 * state_size)], load_sem.at[5 + 3 * s]
            )
        )
    barrier = pltpu.get_barrier_semaphore()
    for mask in range(1, parts):
        pl.semaphore_signal(
            barrier, inc=1, device_id={"mp": xor_place(me, mask)}, device_id_type=MESH
        )
    for k in range(1, shards):
        pl.semaphore_signal(
            barrier, inc=1, device_id={"dp": lax.rem(dp + k, shards)}, device_id_type=MESH
        )
    pl.semaphore_signal(barrier, inc=1, device_id=other_id, device_id_type=MESH)
    for load in loads:
        load.start()
    pl.semaphore_wait(barrier, parts - 1 + shards - 1 + 1)

    def remote(src, dst, send, recv, device):
        return pltpu.make_async_remote_copy(
            src_ref=src,
            dst_ref=dst,
            send_sem=send,
            recv_sem=recv,
            device_id=device,
            device_id_type=MESH,
        )

    def owners(q, side):
        return lax.rem(1 + side + q // chunks, 2)

    def token_rows(q, side):
        return tokens_hbm.at[pl.ds(2 * owners(q, side), 2), lax.rem(q, chunks)]

    def columns(s):
        return pl.ds(s * depth, depth)

    def own_copy(q):
        return pltpu.make_async_copy(
            token_rows(q, side), tok.at[q, :, :, columns(0)], own_sem.at[q]
        )

    def sib_copy(q):
        return remote(
            token_rows(q, side), tok.at[q, :, :, columns(1)], sib_send.at[q], sib_recv.at[q], sib_id
        )

    def far_copy(q):
        return remote(
            token_rows(q, 1 - side),
            tok.at[q, :, :, columns(2)],
            far_send.at[q],
            far_recv.at[q],
            far_id,
        )

    def diag_copy(q):
        return remote(
            tok.at[q, :, :, columns(2)],
            tok.at[q, :, :, columns(3)],
            diag_send.at[q],
            diag_recv.at[q],
            sib_id,
        )

    def store_copy(k):
        return remote(
            outbound.at[pl.ds(k * capacity, capacity)],
            inbound.at[pl.ds(k * capacity, capacity)],
            store_send.at[k],
            store_recv.at[k],
            {"dp": lax.rem(dp + k, shards)},
        )

    def back_copy(k, n):
        there = pl.ds(n * tail, tail)
        return remote(
            outgoing.at[pl.ds(k * capacity, capacity), there],
            returned[n].at[pl.ds(k * capacity, capacity)],
            back_send.at[k, n],
            back_recv.at[k, n],
            {"dp": lax.rem(dp + shards - k, shards)},
        )

    def piece_at(g, k):
        return pl.ds(pl.multiple_of((g * share + k) * height, height), height)

    def piece_copy():
        here = piece_at(group, low)
        return remote(outw.at[0, here], outw.at[2, here], piece_send, piece_recv, far_id)

    def relay_copy(way, step):
        here = piece_at(group, low - way * (step - 1))
        n = 2 * (step - 1) + (way + 1) // 2
        return remote(
            outw.at[2, here],
            outw.at[2, here],
            relay_send.at[n],
            relay_recv.at[n],
            {"dp": dp + way},
        )

    def relay_sends(way, step):
        origin, target = low - way * (step - 1), low + way
        return (origin >= 0) & (origin < share) & (target >= 0) & (target < share)

    def relay_receives(way, step):
        origin = low - way * step
        return (origin >= 0) & (origin < share)

    def relay_start(step):
        for way in (1, -1):

            @pl.when(relay_sends(way, step))
            def _():
                relay_copy(way, step).start()

    def relay_take(step):
        for way in (1, -1):

            @pl.when(relay_receives(way, step))
            def _():
                relay_copy(way, step).wait_recv()
                across_copy(group, low - way * step).start()
                pass_copy(group, low - way * step).start()

    def across_copy(g, k):
        here = piece_at(g, k)
        return remote(
            outw.at[2, here], outw.at[2, here], across_send.at[k], across_recv.at[k], other_id
        )

    def pass_copy(g, k):
        here = piece_at(g, k)
        n = g * share + k
        return remote(outw.at[2, here], outw.at[3, here], pass_send.at[n], pass_recv.at[n], sib_id)

    def whole_copy():
        n = pieces
        return remote(outw.at[0], outw.at[1], pass_send.at[n], pass_recv.at[n], sib_id)

    def norm_copy(s, j):
        if s == 1:
            t, device = 2 * (chunks + j) + 1 - half, sib_id
        elif s == 2:
            t, device = 2 * j + half, far_id
        else:
            t, device = 2 * j + 1 - half, diag_id
        return remote(
            normed.at[t], got.at[s - 1, j], norm_send.at[s - 1, j], norm_recv.at[s - 1, j], device
        )

    ahead = min(3, rounds)
    for q in range(ahead):
        far_copy(q).start()

    loads[0].wait()
    table_ref[...] = slot_tables(home_ref[...], dp, sessions, shards, capacity)
    table_copy = pltpu.make_async_copy(table_ref, table, table_sem)
    table_copy.start()

    @pl.loop(0, rounds)
    def _(q):
        own_copy(q).start()
        sib_copy(q).start()

    lane = lax.broadcasted_iota(jnp.int32, (slots, slots), 1)
    row = lax.broadcasted_iota(jnp.int32, (slots, slots), 0)
    pair = 2 * head_size
    wide = 256
    tall = lax.broadcasted_iota(jnp.int32, (wide, wide), 0)
    flat = lax.broadcasted_iota(jnp.int32, (wide, wide), 1)
    band = wide // sessions
    swap_in = (flat == lax.rem(tall, band) * sessions + tall // band).astype(BF16)
    swap_out = (flat == lax.rem(tall, sessions) * band + tall // sessions).astype(BF16)
    blocks = store_ref.shape[1] // band

    loads[1].wait()

    @pl.loop(0, blocks // 2)
    def _(b):
        def stack(b):
            base = b * (band * 128)
            cuts = [
                raw_store[:, pl.ds(pl.multiple_of(base + a * 128, 128), 128)] for a in range(band)
            ]
            return jnp.concatenate(cuts, axis=0)

        stacked = jnp.concatenate([stack(2 * b), stack(2 * b + 1)], axis=1)
        moved = jnp.dot(swap_in, stacked, preferred_element_type=F32).astype(BF16)
        for n in range(2):
            at = pl.ds(pl.multiple_of((2 * b + n) * band, band), band)
            part = moved[:, n * 128 : (n + 1) * 128]
            store_ref[:, at, :] = part.reshape(sessions, band, 128)

    table_copy.wait()
    for k in range(1, shards):
        for c in range(capacity):
            outbound[k * capacity + c] = store_ref[look(2, k * capacity + c, sessions)]
        store_copy(k).start()
    for c in range(capacity):
        inbound[c] = store_ref[look(2, c, sessions)]

    within = lax.rem(lane, head_size)
    first = within < head_size // 2
    places = row == 2 * within + lane // head_size
    spread = places.astype(BF16)
    back = (lane == 2 * lax.rem(row, head_size) + row // head_size).astype(BF16)
    tile = min(512, model)

    loads[2].wait()

    @pl.loop(0, model // tile)
    def _(t):
        cols = pl.ds(pl.multiple_of(t * tile, tile), tile)
        for g in range(heads // 2):
            part = slice(g * pair, (g + 1) * pair)
            moved = jnp.dot(back, outw[0, part, cols], preferred_element_type=F32)
            outw[0, part, cols] = moved.astype(BF16)

    piece_copy().start()
    whole_copy().start()

    eye = lax.broadcasted_iota(jnp.int32, (heads, heads), 0) == lax.broadcasted_iota(
        jnp.int32, (heads, heads), 1
    )
    rate_col = jnp.sum(jnp.where(eye, rate_ref[...], 0.0), axis=1, keepdims=True)
    bias_col = jnp.sum(jnp.where(eye, bias_ref[...], 0.0), axis=1, keepdims=True)
    causal = row >= lane
    gains = []
    for g in range(heads // 2):
        column = jnp.sum(
            jnp.where(row == lane, gain_ref[:, g * pair : (g + 1) * pair], 0.0),
            axis=1,
            keepdims=True,
        )
        gains.append(jnp.sum(jnp.where(places, column, 0.0), axis=0, keepdims=True))

    for load in loads[3:]:
        load.wait()

    for s in range(parts):
        start = xor_place(me, s) * depth
        for b in range(depth // 128):
            cut = dtw_ref[:, pl.ds(pl.multiple_of(start + b * 128, 128), 128)].astype(F32)
            cut = jnp.concatenate([cut, jnp.zeros((128 - heads, 128), F32)], axis=0)
            at = slice(s * depth + b * 128, s * depth + (b + 1) * 128)
            bd_ref[at, 2 * state_size :] = cut.T.astype(BF16)

    @pl.loop(0, parts)
    def _(t):
        part = pl.ds(pl.multiple_of(t * depth, depth), depth)
        for ref in (x_ref, z_ref):
            for g in range(heads // 2):
                cols = slice(g * pair, (g + 1) * pair)
                moved = jnp.dot(ref[part, cols], spread, preferred_element_type=F32)
                ref[part, cols] = moved.astype(BF16)

    line = lax.broadcasted_iota(jnp.int32, pick_ref.shape, 0)
    spot = lax.broadcasted_iota(jnp.int32, pick_ref.shape, 1)
    fade_spot = spot - heads * 128
    fade_head = 2 * (fade_spot // pair) + jnp.where(
        lax.rem(fade_spot, head_size) < head_size // 2, 0, 1
    )
    for_cum = (spot < heads * 128) & (line < 3 * heads) & (lax.rem(line, heads) == spot // 128)
    for_fade = (spot >= heads * 128) & (line >= 3 * heads) & (line < 5 * heads)
    for_fade = for_fade & (lax.rem(line, heads) == fade_head)
    pick_ref[...] = jnp.where(for_cum | for_fade, 1.0, 0.0).astype(BF16)

    def terms(value, n):
        found = []
        for _ in range(n):
            found.append(value.astype(BF16).astype(F32))
            value = value - found[-1]
        return found

    def prepare(q, raw):
        raw = raw.T[:heads]
        raw = jnp.concatenate([raw[:, :slots] + bias_col, raw[:, slots:] + bias_col], axis=0)
        limits = [
            jnp.full((heads, slots), counts[session_of(q, o)], jnp.int32) for o in range(2)
        ]
        lane8 = lax.broadcasted_iota(jnp.int32, (2 * heads, slots), 1)
        dt_t = jnp.maximum(raw, 0.0) + jnp.log1p(jnp.exp(-jnp.abs(raw)))
        dt_t = jnp.where(lane8 < jnp.concatenate(limits, axis=0), dt_t, 0.0)
        cum_t = dt_t * jnp.concatenate([rate_col, rate_col], axis=0)
        shift = 1
        while shift < slots:
            moved = pltpu.roll(cum_t, shift, axis=1)
            cum_t = cum_t + jnp.where(lane8 >= shift, moved, 0.0)
            shift *= 2
        last = cum_t[:, slots - 1 : slots]
        weigh_t = jnp.exp(cum_t - last) * dt_t
        fade_t = jnp.exp(-cum_t)
        keep_t = jnp.broadcast_to(fade_t[:, slots - 1 : slots], fade_t.shape)
        for o in range(2):
            part = slice(o * heads, (o + 1) * heads)
            rows_ref[2 * q + o] = jnp.concatenate(
                [value[part] for value in (cum_t, dt_t, weigh_t, keep_t)], axis=0
            )
            table_t = terms(cum_t[part], 3) + terms(fade_t[part], 2)
            table_t.append(jnp.zeros((128 - 5 * heads, slots), F32))
            cols_ref[2 * q + o] = jnp.concatenate(table_t, axis=0).T.astype(BF16)

    def session_of(q, o):
        return (2 * owners(q, side) + o) * chunks + lax.rem(q, chunks)

    def split_heads(t, g):
        xs = xs_ref[t, :, g * pair : (g + 1) * pair]
        none = jnp.zeros((), BF16)
        return jnp.concatenate([jnp.where(first, xs, none), jnp.where(first, none, xs)], axis=0)

    def states(q, o):
        t = 2 * q + o
        index = session_of(q, o)
        spot = look(0, index, shards * capacity)
        rows_t = rows_ref[t]
        b_t = bc_ref[t].astype(F32).T[:state_size]
        for g in range(heads // 2):
            part = slice(g * head_size, (g + 1) * head_size)
            weighed = [
                (b_t * rows_t[2 * heads + h : 2 * heads + h + 1]).astype(BF16)
                for h in (2 * g, 2 * g + 1)
            ]
            grown = jnp.dot(
                jnp.concatenate(weighed, axis=1), split_heads(t, g), preferred_element_type=F32
            ).T
            grown = jnp.concatenate([grown[:head_size], grown[head_size:]], axis=1)
            keep = jnp.where(
                row[:head_size] < head_size // 2,
                rows_t[3 * heads + 2 * g : 3 * heads + 2 * g + 1],
                rows_t[3 * heads + 2 * g + 1 : 3 * heads + 2 * g + 2],
            )
            kept = inbound[spot, part, :].astype(F32)
            state_ref[index, part, :] = (keep * kept + grown).astype(BF16)

    def outputs(q, o):
        t = 2 * q + o
        index = session_of(q, o)
        count = counts[index]
        spot = look(0, index, shards * capacity)
        rows_t = rows_ref[t]
        cols_t = cols_ref[t]
        b_bf = bc_ref[t, :, :state_size]
        c_bf = bc_ref[t, :, state_size:]
        scores = lax.dot_general(
            c_bf, b_bf, (((1,), (1,)), ((), ())), preferred_element_type=F32
        )
        gated_parts = []
        squares = None
        for g in range(heads // 2):
            mixes = []
            ends = jnp.dot(
                cols_t, pick_ref[:, g * 256 : (g + 1) * 256], preferred_element_type=F32
            )
            for h in (2 * g, 2 * g + 1):
                end = ends[:, (h % 2) * 128 : (h % 2 + 1) * 128]
                gaps = jnp.where(causal, rows_t[h : h + 1] - end, -1e30)
                mixes.append(
                    (jnp.exp(gaps) * rows_t[heads + h : heads + h + 1] * scores).astype(BF16)
                )
            y = jnp.dot(
                jnp.concatenate(mixes, axis=1), split_heads(t, g), preferred_element_type=F32
            )
            kept = inbound[spot, g * head_size : (g + 1) * head_size, :]
            halves = jnp.concatenate([kept[:, :state_size], kept[:, state_size:]], axis=0)
            carried = lax.dot_general(
                c_bf, halves, (((1,), (1,)), ((), ())), preferred_element_type=F32
            )
            at = heads * 128 + g * pair
            fades = jnp.dot(cols_t, pick_ref[:, at : at + pair], preferred_element_type=F32)
            y = y + carried * fades
            zs = zs_ref[t, :, g * pair : (g + 1) * pair].astype(F32)
            gated = y * (zs * jax.nn.sigmoid(zs))
            square = gated * gated
            squares = square if squares is None else squares + square
            gated_parts.append(gated)
        squares = jnp.sum(squares, axis=1, keepdims=True)
        scale = lax.rsqrt(squares * (1.0 / inner) + 1e-05)
        scale = jnp.where(row[:, :1] < count, scale, 0.0)
        for g in range(heads // 2):
            cols = slice(g * pair, (g + 1) * pair)
            normed[t, :, cols] = (gated_parts[g] * scale * gains[g]).astype(BF16)

    def project(q):
        own_copy(q).wait()
        sib_copy(q).wait_recv()
        diag_copy(q).wait_recv()
        values = tok[q].reshape(rows, parts * depth)
        at = pl.ds(2 * q, 2)
        total = jnp.dot(values, bd_ref[...], preferred_element_type=F32)
        bc_ref[at] = total[:, : 2 * state_size].astype(BF16).reshape(2, slots, 2 * state_size)
        prepare(q, total[:, 2 * state_size :])
        total = jnp.dot(values, x_ref[...], preferred_element_type=F32)
        xs_ref[at] = total.astype(BF16).reshape(2, slots, inner)

    def project_gates(q):
        values = tok[q].reshape(rows, parts * depth)
        total = jnp.dot(values, z_ref[...], preferred_element_type=F32)
        zs_ref[pl.ds(2 * q, 2)] = total.astype(BF16).reshape(2, slots, inner)

    def reached(q):
        return jnp.where(q < lag, 0, jnp.minimum(2 * (q - lag + 1), q + 1))

    def round_trip(q, carry):
        far_copy(q).wait_recv()
        diag_copy(q).start()

        @pl.when(q + ahead < rounds)
        def _():
            far_copy(q + ahead).start()

        @pl.when(q == 1)
        def _():
            piece_copy().wait_recv()
            across_copy(group, low).start()
            pass_copy(group, low).start()
            relay_start(1)

        for step in range(1, share):

            @pl.when(q == min(1 + 2 * step, rounds - 1))
            def _():
                relay_take(step)
                if step + 1 < share:
                    relay_start(step + 1)

        @pl.when(q == rounds - 1)
        def _():
            for j in range(chunks // 2):
                norm_copy(2, j).start()
                norm_copy(3, j).start()

        project(q)

        @pl.when(q == lag)
        def _():
            for k in range(1, shards):
                store_copy(k).wait_recv()

        @pl.loop(reached(q - 1), reached(q))
        def _(done):
            states(done, 0)
            states(done, 1)

        @pl.when(q == rounds - 1)
        def _():
            for k in range(1, shards):
                for c in range(capacity):
                    outgoing[k * capacity + c] = state_ref[look(3, k * capacity + c, sessions)]
            for n in range(2):
                for k in range(1, shards):
                    back_copy(k, n).start()

        project_gates(q)

        @pl.loop(reached(q - 1), reached(q))
        def _(done):
            outputs(done, 0)
            outputs(done, 1)

        return carry

    lax.fori_loop(0, rounds, round_trip, 0)

    for j in range(chunks):
        norm_copy(1, j).start()
    for c in range(capacity):
        for n in range(2):
            there = slice(n * tail, (n + 1) * tail)
            returned[n][c] = state_ref[look(3, c, sessions), there, :]

    whole_copy().wait_recv()
    for j in range(chunks):
        norm_copy(1, j).wait_recv()

    @pl.loop(0, model // tile)
    def _(t):
        cols = pl.ds(pl.multiple_of(t * tile, tile), tile)
        mine = jnp.concatenate([normed[2 * (chunks + j) + half] for j in range(chunks)], axis=0)
        total = jnp.dot(mine, outw[0, :, cols], preferred_element_type=F32)
        theirs = got[0].reshape(chunks * slots, inner)
        total += jnp.dot(theirs, outw[1, :, cols], preferred_element_type=F32)
        sums[:, :, cols] = total.reshape(chunks, slots, tile)

    for j in range(chunks // 2):
        norm_copy(2, j).wait_send()
        norm_copy(2, j + chunks // 2).start()
        norm_copy(3, j).wait_send()
        norm_copy(3, j + chunks // 2).start()
    for k in range(share):
        across_copy(1 - group, k).wait_recv()
        pass_copy(1 - group, k).start()
    for k in range(share):
        for g in range(2):
            pass_copy(g, k).wait_recv()

    for n in range(2):
        span = slice(n * chunks // 2, (n + 1) * chunks // 2)
        for j in range(span.start, span.stop):
            norm_copy(2, j).wait_recv()
            norm_copy(3, j).wait_recv()

        @pl.loop(0, model // tile)
        def _(t):
            cols = pl.ds(pl.multiple_of(t * tile, tile), tile)
            total = sums[span, :, cols].reshape(chunks // 2 * slots, tile)
            for s in (2, 3):
                total += jnp.dot(
                    got[s - 1, span].reshape(chunks // 2 * slots, inner),
                    outw[s, :, cols],
                    preferred_element_type=F32,
                )
            out_ref[span.start * slots : span.stop * slots, cols] = total.astype(BF16)

        for k in range(1, shards):
            back_copy(k, n).wait_recv()

        where = [look(1, r, shards * capacity) for r in range(sessions)]

        @pl.loop(0, blocks // 4)
        def _(b):
            def stack(b):
                at = pl.ds(pl.multiple_of(b * band, band), band)
                return jnp.concatenate([returned[n][spot, at, :] for spot in where], axis=0)

            found = jnp.concatenate([stack(2 * b), stack(2 * b + 1)], axis=1)
            moved = jnp.dot(swap_out, found, preferred_element_type=F32).astype(BF16)
            for m in range(2):
                base = (n * (blocks // 2) + 2 * b + m) * (band * 128)
                for a in range(band):
                    new_store_ref[:, pl.ds(pl.multiple_of(base + a * 128, 128), 128)] = moved[
                        a * sessions : (a + 1) * sessions, m * 128 : (m + 1) * 128
                    ]

    @pl.loop(0, rounds)
    def _(q):
        far_copy(q).wait_send()
        sib_copy(q).wait_send()
        diag_copy(q).wait_send()

    for j in range(chunks):
        norm_copy(1, j).wait_send()
    for j in range(chunks // 2, chunks):
        norm_copy(2, j).wait_send()
        norm_copy(3, j).wait_send()
    for k in range(1, shards):
        store_copy(k).wait_send()
        for n in range(2):
            back_copy(k, n).wait_send()
    piece_copy().wait_send()
    whole_copy().wait_send()
    for k in range(share):
        across_copy(group, k).wait_send()
        for g in range(2):
            pass_copy(g, k).wait_send()
    for step in range(1, share):
        for way in (1, -1):

            @pl.when(relay_sends(way, step))
            def _():
                relay_copy(way, step).wait_send()


def run_layer(counts, home, tokens4, store, weights, params, out_weight, sizes, shards, capacity):
    heads, head_size, state_size = sizes
    parts, chunks, slots, depth = tokens4.shape
    x_weight, z_weight, bc_weight, dt_weight = weights
    inner = heads * head_size
    model = out_weight.shape[1]
    sessions, state_width = store.shape
    share = min(4, shards)
    pieces = 2 * share
    rounds = 2 * chunks
    vmem = pl.BlockSpec(memory_space=pltpu.VMEM)
    hbm = pl.BlockSpec(memory_space=pl.ANY)
    dma = pltpu.SemaphoreType.DMA
    state = (state_width // 128, 128)
    exchange = pltpu.VMEM((shards * capacity,) + state, BF16)
    piece = pltpu.VMEM((shards * capacity, state[0] // 2, state[1]), BF16)
    kept = pltpu.VMEM((sessions,) + state, BF16)
    width = parts * depth
    return pl.pallas_call(
        functools.partial(
            layer_kernel, heads, head_size, state_size, chunks, parts, shards, share, capacity
        ),
        out_shape=(
            pltpu.VMEM((chunks * slots, model), BF16),
            pltpu.VMEM(store.shape, BF16),
        ),
        in_specs=[pl.BlockSpec(memory_space=pltpu.SMEM)] + [hbm] * 6 + [vmem] * 4 + [hbm],
        out_specs=(vmem, vmem),
        scratch_shapes=[
            pltpu.VMEM((width, inner), BF16),
            pltpu.VMEM((width, inner), BF16),
            pltpu.VMEM((width, 2 * state_size + 128), BF16),
            pltpu.VMEM((parts, inner, model), BF16),
            pltpu.VMEM((rounds, 2, slots, width), BF16),
            pltpu.VMEM(home.shape, jnp.int32),
            pltpu.VMEM((8, 128), jnp.int32),
            pltpu.SMEM((8, 128), jnp.int32),
            pltpu.VMEM(store.shape, BF16),
            kept,
            exchange,
            exchange,
            kept,
            exchange,
            piece,
            piece,
            pltpu.VMEM((sessions, slots, inner), BF16),
            pltpu.VMEM((sessions, slots, inner), BF16),
            pltpu.VMEM((sessions, slots, 2 * state_size), BF16),
            pltpu.VMEM((sessions, 4 * heads, slots), F32),
            pltpu.VMEM((sessions, slots, 128), BF16),
            pltpu.VMEM((128, heads * 128 + inner), BF16),
            pltpu.VMEM((sessions, slots, inner), BF16),
            pltpu.VMEM((parts - 1, chunks, slots, inner), BF16),
            pltpu.VMEM((chunks, slots, model), F32),
            dma((3 + 3 * parts,)),
            dma,
        ]
        + [dma((rounds,))] * 7
        + [dma((shards,))] * 2
        + [dma((shards, 2))] * 2
        + [dma, dma]
        + [dma((2 * share,))] * 2
        + [dma((share,))] * 2
        + [dma((pieces + 1,))] * 2
        + [dma((parts - 1, chunks))] * 2,
        compiler_params=pltpu.CompilerParams(
            vmem_limit_bytes=56 * 1024 * 1024, collective_id=0, has_side_effects=True
        ),
        cost_estimate=pl.CostEstimate(
            flops=2 * sessions * slots * width * (2 * inner + 256 + model // parts),
            bytes_accessed=16 * 1024 * 1024,
            transcendentals=sessions * slots * heads * slots,
        ),
        name="layer",
    )(
        counts,
        home,
        tokens4,
        store,
        x_weight,
        z_weight,
        bc_weight,
        dt_weight.T,
        *params,
        out_weight,
    )


def body(
    tokens,
    x_weight,
    z_weight,
    bc_weight,
    dt_weight,
    dt_bias,
    decay_rate,
    norm_gain,
    out_weight,
    store_states,
    home_rows,
    event_counts,
):
    shards = lax.axis_size("dp")
    parts = lax.axis_size("mp")
    sessions = store_states.shape[0]
    capacity = max(2, (sessions + shards - 1) // shards)
    heads = dt_bias.shape[0]
    inner = x_weight.shape[1]
    state_size = bc_weight.shape[1] // 2
    slots = tokens.shape[0] // sessions
    tokens4 = tokens.reshape(parts, sessions // parts, slots, tokens.shape[1])
    return run_layer(
        event_counts,
        home_rows[None, :],
        tokens4,
        store_states,
        (x_weight, z_weight, bc_weight, dt_weight),
        (dt_bias[None, :], decay_rate[None, :], norm_gain[None, :]),
        out_weight,
        (heads, inner // heads, state_size),
        shards,
        capacity,
    )


def solution(mesh):
    return jax.shard_map(
        body,
        mesh=mesh,
        in_specs=(
            P(("groups", "dp"), "mp"),
            P(None, "mp"),
            P(None, "mp"),
            P(None, "mp"),
            P(None, "mp"),
            P("mp"),
            P("mp"),
            P("mp"),
            P("mp", None),
            P(("groups", "dp"), "mp"),
            P("groups"),
            P(("groups", "dp")),
        ),
        out_specs=(P(("groups", "dp", "mp"), None), P(("groups", "dp"), "mp")),
        check_vma=False,
    )
```

```python
import functools

import jax
import jax.numpy as jnp
from jax import lax
from jax.experimental import pallas as pl
from jax.experimental.pallas import tpu as pltpu
from jax.sharding import PartitionSpec as P

F32 = jnp.float32
BF16 = jnp.bfloat16
MESH = pl.DeviceIdType.MESH


def xor_place(me, mask):
    return lax.rem(lax.rem(me, 2) + mask % 2, 2) + 2 * lax.rem(me // 2 + mask // 2, 2)


def wrap(value, size):
    return jnp.where(value >= size, value - size, value)


def slot_tables(home, dp, sessions, shards, capacity):
    total = home.shape[1]
    base = (dp * sessions).astype(F32)
    here = dp.astype(F32)
    home = home.astype(F32)
    who = lax.broadcasted_iota(jnp.int32, (sessions, total), 1).astype(F32)
    spot = lax.broadcasted_iota(jnp.int32, (sessions, total), 0).astype(F32) + base
    owner = jnp.sum(jnp.where(home == spot, who, 0.0), axis=1, keepdims=True)
    wanted = jnp.sum(jnp.where(who == spot, home, 0.0), axis=1, keepdims=True)
    server = jnp.floor(owner * (1.0 / sessions))
    shard = jnp.floor(wanted * (1.0 / sessions))
    place = lax.broadcasted_iota(jnp.int32, (sessions, 128), 0).astype(F32)
    lane = lax.broadcasted_iota(jnp.int32, (sessions, 128), 1).astype(F32)

    def as_row(column):
        return jnp.sum(jnp.where(place == lane, column, 0.0), axis=0, keepdims=True)

    def rank(keys, order):
        earlier = (as_row(keys) == keys) & (as_row(order) < order) & (lane < sessions)
        return jnp.sum(jnp.where(earlier, 1.0, 0.0), axis=1, keepdims=True)

    to_server = wrap(server - here + shards, shards)
    from_home = wrap(here - shard + shards, shards)
    row_slot = to_server * capacity + rank(server, place[:, :1])
    session_slot = from_home * capacity + rank(shard, wanted - shard * sessions)

    def holder(slots):
        return jnp.sum(jnp.where(slots == lane, place, 0.0), axis=0, keepdims=True)

    rows = [as_row(session_slot), as_row(row_slot), holder(row_slot), holder(session_slot)]
    return jnp.concatenate(rows + [jnp.zeros((4, 128), F32)], axis=0).astype(jnp.int32)


def layer_kernel(
    heads,
    head_size,
    state_size,
    chunks,
    parts,
    shards,
    share,
    capacity,
    counts,
    home_hbm,
    tokens_hbm,
    store_hbm,
    x_hbm,
    z_hbm,
    bc_hbm,
    dtw_ref,
    bias_ref,
    rate_ref,
    gain_ref,
    outw_hbm,
    out_ref,
    new_store_ref,
    x_ref,
    z_ref,
    bd_ref,
    outw,
    tok,
    home_ref,
    table_ref,
    table,
    raw_store,
    store_ref,
    outbound,
    inbound,
    state_ref,
    outgoing,
    upper,
    lower,
    xs_ref,
    zs_ref,
    bc_ref,
    rows_ref,
    cols_ref,
    pick_ref,
    normed,
    got,
    sums,
    load_sem,
    table_sem,
    own_sem,
    sib_send,
    sib_recv,
    far_send,
    far_recv,
    diag_send,
    diag_recv,
    store_send,
    store_recv,
    back_send,
    back_recv,
    piece_send,
    piece_recv,
    relay_send,
    relay_recv,
    across_send,
    across_recv,
    pass_send,
    pass_recv,
    norm_send,
    norm_recv,
):
    slots = tokens_hbm.shape[2]
    depth = tokens_hbm.shape[3]
    model = outw_hbm.shape[1]
    inner = heads * head_size
    sessions = chunks * parts
    rounds = 2 * chunks
    lag = max(1, rounds // 2 - 1)
    rows = 2 * slots
    me = lax.axis_index("mp")
    dp = lax.axis_index("dp")
    group = lax.axis_index("groups")
    half = lax.rem(me, 2)
    side = me // 2
    low = lax.rem(dp, share)
    pieces = 2 * share
    height = inner // pieces
    sib_id = {"mp": xor_place(me, 1)}
    far_id = {"mp": xor_place(me, 2)}
    diag_id = {"mp": xor_place(me, 3)}
    tail = state_ref.shape[1] // 2
    returned = (upper, lower)
    other_id = {"groups": 1 - group}

    def look(line, at, size):
        return jnp.minimum(jnp.maximum(table[line, at], 0), size - 1)

    loads = [
        pltpu.make_async_copy(home_hbm, home_ref, load_sem.at[0]),
        pltpu.make_async_copy(store_hbm, raw_store, load_sem.at[1]),
        pltpu.make_async_copy(outw_hbm, outw.at[0], load_sem.at[2]),
    ]
    for s in range(parts):
        part = pl.ds(pl.multiple_of(xor_place(me, s) * depth, depth), depth)
        there = pl.ds(s * depth, depth)
        loads.append(pltpu.make_async_copy(x_hbm.at[part], x_ref.at[there], load_sem.at[3 + 3 * s]))
        loads.append(pltpu.make_async_copy(z_hbm.at[part], z_ref.at[there], load_sem.at[4 + 3 * s]))
        loads.append(
            pltpu.make_async_copy(
                bc_hbm.at[part], bd_ref.at[there, pl.ds(0, 2 * state_size)], load_sem.at[5 + 3 * s]
            )
        )
    barrier = pltpu.get_barrier_semaphore()
    for mask in range(1, parts):
        pl.semaphore_signal(
            barrier, inc=1, device_id={"mp": xor_place(me, mask)}, device_id_type=MESH
        )
    for k in range(1, shards):
        pl.semaphore_signal(
            barrier, inc=1, device_id={"dp": lax.rem(dp + k, shards)}, device_id_type=MESH
        )
    pl.semaphore_signal(barrier, inc=1, device_id=other_id, device_id_type=MESH)
    for load in loads:
        load.start()
    pl.semaphore_wait(barrier, parts - 1 + shards - 1 + 1)

    def remote(src, dst, send, recv, device):
        return pltpu.make_async_remote_copy(
            src_ref=src,
            dst_ref=dst,
            send_sem=send,
            recv_sem=recv,
            device_id=device,
            device_id_type=MESH,
        )

    def owners(q, side):
        return lax.rem(1 + side + q // chunks, 2)

    def token_rows(q, side):
        return tokens_hbm.at[pl.ds(2 * owners(q, side), 2), lax.rem(q, chunks)]

    def columns(s):
        return pl.ds(s * depth, depth)

    def own_copy(q):
        return pltpu.make_async_copy(
            token_rows(q, side), tok.at[q, :, :, columns(0)], own_sem.at[q]
        )

    def sib_copy(q):
        return remote(
            token_rows(q, side), tok.at[q, :, :, columns(1)], sib_send.at[q], sib_recv.at[q], sib_id
        )

    def far_copy(q):
        return remote(
            token_rows(q, 1 - side),
            tok.at[q, :, :, columns(2)],
            far_send.at[q],
            far_recv.at[q],
            far_id,
        )

    def diag_copy(q):
        return remote(
            tok.at[q, :, :, columns(2)],
            tok.at[q, :, :, columns(3)],
            diag_send.at[q],
            diag_recv.at[q],
            sib_id,
        )

    def store_copy(k):
        return remote(
            outbound.at[pl.ds(k * capacity, capacity)],
            inbound.at[pl.ds(k * capacity, capacity)],
            store_send.at[k],
            store_recv.at[k],
            {"dp": lax.rem(dp + k, shards)},
        )

    def back_copy(k, n):
        there = pl.ds(n * tail, tail)
        return remote(
            outgoing.at[pl.ds(k * capacity, capacity), there],
            returned[n].at[pl.ds(k * capacity, capacity)],
            back_send.at[k, n],
            back_recv.at[k, n],
            {"dp": lax.rem(dp + shards - k, shards)},
        )

    def piece_at(g, k):
        return pl.ds(pl.multiple_of((g * share + k) * height, height), height)

    def piece_copy():
        here = piece_at(group, low)
        return remote(outw.at[0, here], outw.at[2, here], piece_send, piece_recv, far_id)

    def relay_copy(way, step):
        here = piece_at(group, low - way * (step - 1))
        n = 2 * (step - 1) + (way + 1) // 2
        return remote(
            outw.at[2, here],
            outw.at[2, here],
            relay_send.at[n],
            relay_recv.at[n],
            {"dp": dp + way},
        )

    def relay_sends(way, step):
        origin, target = low - way * (step - 1), low + way
        return (origin >= 0) & (origin < share) & (target >= 0) & (target < share)

    def relay_receives(way, step):
        origin = low - way * step
        return (origin >= 0) & (origin < share)

    def relay_start(step):
        for way in (1, -1):

            @pl.when(relay_sends(way, step))
            def _():
                relay_copy(way, step).start()

    def relay_take(step):
        for way in (1, -1):

            @pl.when(relay_receives(way, step))
            def _():
                relay_copy(way, step).wait_recv()
                across_copy(group, low - way * step).start()
                pass_copy(group, low - way * step).start()

    def across_copy(g, k):
        here = piece_at(g, k)
        return remote(
            outw.at[2, here], outw.at[2, here], across_send.at[k], across_recv.at[k], other_id
        )

    def pass_copy(g, k):
        here = piece_at(g, k)
        n = g * share + k
        return remote(outw.at[2, here], outw.at[3, here], pass_send.at[n], pass_recv.at[n], sib_id)

    def whole_copy():
        n = pieces
        return remote(outw.at[0], outw.at[1], pass_send.at[n], pass_recv.at[n], sib_id)

    def norm_copy(s, j):
        if s == 1:
            t, device = 2 * (chunks + j) + 1 - half, sib_id
        elif s == 2:
            t, device = 2 * j + half, far_id
        else:
            t, device = 2 * j + 1 - half, diag_id
        return remote(
            normed.at[t], got.at[s - 1, j], norm_send.at[s - 1, j], norm_recv.at[s - 1, j], device
        )

    ahead = min(3, rounds)
    for q in range(ahead):
        far_copy(q).start()

    loads[0].wait()
    table_ref[...] = slot_tables(home_ref[...], dp, sessions, shards, capacity)
    table_copy = pltpu.make_async_copy(table_ref, table, table_sem)
    table_copy.start()

    @pl.loop(0, rounds)
    def _(q):
        own_copy(q).start()
        sib_copy(q).start()

    lane = lax.broadcasted_iota(jnp.int32, (slots, slots), 1)
    row = lax.broadcasted_iota(jnp.int32, (slots, slots), 0)
    pair = 2 * head_size
    wide = 256
    tall = lax.broadcasted_iota(jnp.int32, (wide, wide), 0)
    flat = lax.broadcasted_iota(jnp.int32, (wide, wide), 1)
    band = wide // sessions
    swap_in = (flat == lax.rem(tall, band) * sessions + tall // band).astype(BF16)
    swap_out = (flat == lax.rem(tall, sessions) * band + tall // sessions).astype(BF16)
    blocks = store_ref.shape[1] // band

    loads[1].wait()

    @pl.loop(0, blocks // 2)
    def _(b):
        def stack(b):
            base = b * (band * 128)
            cuts = [
                raw_store[:, pl.ds(pl.multiple_of(base + a * 128, 128), 128)] for a in range(band)
            ]
            return jnp.concatenate(cuts, axis=0)

        stacked = jnp.concatenate([stack(2 * b), stack(2 * b + 1)], axis=1)
        moved = jnp.dot(swap_in, stacked, preferred_element_type=F32).astype(BF16)
        for n in range(2):
            at = pl.ds(pl.multiple_of((2 * b + n) * band, band), band)
            part = moved[:, n * 128 : (n + 1) * 128]
            store_ref[:, at, :] = part.reshape(sessions, band, 128)

    table_copy.wait()
    for k in range(1, shards):
        for c in range(capacity):
            outbound[k * capacity + c] = store_ref[look(2, k * capacity + c, sessions)]
        store_copy(k).start()
    for c in range(capacity):
        inbound[c] = store_ref[look(2, c, sessions)]

    within = lax.rem(lane, head_size)
    first = within < head_size // 2
    places = row == 2 * within + lane // head_size
    spread = places.astype(BF16)
    back = (lane == 2 * lax.rem(row, head_size) + row // head_size).astype(BF16)
    tile = min(512, model)

    loads[2].wait()

    @pl.loop(0, model // tile)
    def _(t):
        cols = pl.ds(pl.multiple_of(t * tile, tile), tile)
        for g in range(heads // 2):
            part = slice(g * pair, (g + 1) * pair)
            moved = jnp.dot(back, outw[0, part, cols], preferred_element_type=F32)
            outw[0, part, cols] = moved.astype(BF16)

    piece_copy().start()
    whole_copy().start()

    eye = lax.broadcasted_iota(jnp.int32, (heads, heads), 0) == lax.broadcasted_iota(
        jnp.int32, (heads, heads), 1
    )
    rate_col = jnp.sum(jnp.where(eye, rate_ref[...], 0.0), axis=1, keepdims=True)
    bias_col = jnp.sum(jnp.where(eye, bias_ref[...], 0.0), axis=1, keepdims=True)
    causal = row >= lane
    gains = []
    for g in range(heads // 2):
        column = jnp.sum(
            jnp.where(row == lane, gain_ref[:, g * pair : (g + 1) * pair], 0.0),
            axis=1,
            keepdims=True,
        )
        gains.append(jnp.sum(jnp.where(places, column, 0.0), axis=0, keepdims=True))

    for load in loads[3:]:
        load.wait()

    for s in range(parts):
        start = xor_place(me, s) * depth
        for b in range(depth // 128):
            cut = dtw_ref[:, pl.ds(pl.multiple_of(start + b * 128, 128), 128)].astype(F32)
            cut = jnp.concatenate([cut, jnp.zeros((128 - heads, 128), F32)], axis=0)
            at = slice(s * depth + b * 128, s * depth + (b + 1) * 128)
            bd_ref[at, 2 * state_size :] = cut.T.astype(BF16)

    @pl.loop(0, parts)
    def _(t):
        part = pl.ds(pl.multiple_of(t * depth, depth), depth)
        for ref in (x_ref, z_ref):
            for g in range(heads // 2):
                cols = slice(g * pair, (g + 1) * pair)
                moved = jnp.dot(ref[part, cols], spread, preferred_element_type=F32)
                ref[part, cols] = moved.astype(BF16)

    line = lax.broadcasted_iota(jnp.int32, pick_ref.shape, 0)
    spot = lax.broadcasted_iota(jnp.int32, pick_ref.shape, 1)
    fade_spot = spot - heads * 128
    fade_head = 2 * (fade_spot // pair) + jnp.where(
        lax.rem(fade_spot, head_size) < head_size // 2, 0, 1
    )
    for_cum = (spot < heads * 128) & (line < 3 * heads) & (lax.rem(line, heads) == spot // 128)
    for_fade = (spot >= heads * 128) & (line >= 3 * heads) & (line < 5 * heads)
    for_fade = for_fade & (lax.rem(line, heads) == fade_head)
    pick_ref[...] = jnp.where(for_cum | for_fade, 1.0, 0.0).astype(BF16)

    def terms(value, n):
        found = []
        for _ in range(n):
            found.append(value.astype(BF16).astype(F32))
            value = value - found[-1]
        return found

    def prepare(q, raw):
        raw = raw.T[:heads]
        raw = jnp.concatenate([raw[:, :slots] + bias_col, raw[:, slots:] + bias_col], axis=0)
        limits = [
            jnp.full((heads, slots), counts[session_of(q, o)], jnp.int32) for o in range(2)
        ]
        lane8 = lax.broadcasted_iota(jnp.int32, (2 * heads, slots), 1)
        dt_t = jnp.maximum(raw, 0.0) + jnp.log1p(jnp.exp(-jnp.abs(raw)))
        dt_t = jnp.where(lane8 < jnp.concatenate(limits, axis=0), dt_t, 0.0)
        cum_t = dt_t * jnp.concatenate([rate_col, rate_col], axis=0)
        shift = 1
        while shift < slots:
            moved = pltpu.roll(cum_t, shift, axis=1)
            cum_t = cum_t + jnp.where(lane8 >= shift, moved, 0.0)
            shift *= 2
        last = cum_t[:, slots - 1 : slots]
        weigh_t = jnp.exp(cum_t - last) * dt_t
        fade_t = jnp.exp(-cum_t)
        keep_t = jnp.broadcast_to(fade_t[:, slots - 1 : slots], fade_t.shape)
        for o in range(2):
            part = slice(o * heads, (o + 1) * heads)
            rows_ref[2 * q + o] = jnp.concatenate(
                [value[part] for value in (cum_t, dt_t, weigh_t, keep_t)], axis=0
            )
            table_t = terms(cum_t[part], 3) + terms(fade_t[part], 2)
            table_t.append(jnp.zeros((128 - 5 * heads, slots), F32))
            cols_ref[2 * q + o] = jnp.concatenate(table_t, axis=0).T.astype(BF16)

    def session_of(q, o):
        return (2 * owners(q, side) + o) * chunks + lax.rem(q, chunks)

    def split_heads(t, g):
        xs = xs_ref[t, :, g * pair : (g + 1) * pair]
        none = jnp.zeros((), BF16)
        return jnp.concatenate([jnp.where(first, xs, none), jnp.where(first, none, xs)], axis=0)

    def states(q, o):
        t = 2 * q + o
        index = session_of(q, o)
        spot = look(0, index, shards * capacity)
        rows_t = rows_ref[t]
        b_t = bc_ref[t].astype(F32).T[:state_size]
        for g in range(heads // 2):
            part = slice(g * head_size, (g + 1) * head_size)
            weighed = [
                (b_t * rows_t[2 * heads + h : 2 * heads + h + 1]).astype(BF16)
                for h in (2 * g, 2 * g + 1)
            ]
            grown = jnp.dot(
                jnp.concatenate(weighed, axis=1), split_heads(t, g), preferred_element_type=F32
            ).T
            grown = jnp.concatenate([grown[:head_size], grown[head_size:]], axis=1)
            keep = jnp.where(
                row[:head_size] < head_size // 2,
                rows_t[3 * heads + 2 * g : 3 * heads + 2 * g + 1],
                rows_t[3 * heads + 2 * g + 1 : 3 * heads + 2 * g + 2],
            )
            kept = inbound[spot, part, :].astype(F32)
            state_ref[index, part, :] = (keep * kept + grown).astype(BF16)

    def outputs(q, o):
        t = 2 * q + o
        index = session_of(q, o)
        count = counts[index]
        spot = look(0, index, shards * capacity)
        rows_t = rows_ref[t]
        cols_t = cols_ref[t]
        b_bf = bc_ref[t, :, :state_size]
        c_bf = bc_ref[t, :, state_size:]
        scores = lax.dot_general(
            c_bf, b_bf, (((1,), (1,)), ((), ())), preferred_element_type=F32
        )
        gated_parts = []
        squares = None
        for g in range(heads // 2):
            mixes = []
            ends = jnp.dot(
                cols_t, pick_ref[:, g * 256 : (g + 1) * 256], preferred_element_type=F32
            )
            for h in (2 * g, 2 * g + 1):
                end = ends[:, (h % 2) * 128 : (h % 2 + 1) * 128]
                gaps = jnp.where(causal, rows_t[h : h + 1] - end, -1e30)
                mixes.append(
                    (jnp.exp(gaps) * rows_t[heads + h : heads + h + 1] * scores).astype(BF16)
                )
            y = jnp.dot(
                jnp.concatenate(mixes, axis=1), split_heads(t, g), preferred_element_type=F32
            )
            kept = inbound[spot, g * head_size : (g + 1) * head_size, :]
            halves = jnp.concatenate([kept[:, :state_size], kept[:, state_size:]], axis=0)
            carried = lax.dot_general(
                c_bf, halves, (((1,), (1,)), ((), ())), preferred_element_type=F32
            )
            at = heads * 128 + g * pair
            fades = jnp.dot(cols_t, pick_ref[:, at : at + pair], preferred_element_type=F32)
            y = y + carried * fades
            zs = zs_ref[t, :, g * pair : (g + 1) * pair].astype(F32)
            gated = y * (zs * jax.nn.sigmoid(zs))
            square = gated * gated
            squares = square if squares is None else squares + square
            gated_parts.append(gated)
        squares = jnp.sum(squares, axis=1, keepdims=True)
        scale = lax.rsqrt(squares * (1.0 / inner) + 1e-05)
        scale = jnp.where(row[:, :1] < count, scale, 0.0)
        for g in range(heads // 2):
            cols = slice(g * pair, (g + 1) * pair)
            normed[t, :, cols] = (gated_parts[g] * scale * gains[g]).astype(BF16)

    def project(q):
        own_copy(q).wait()
        sib_copy(q).wait_recv()
        diag_copy(q).wait_recv()
        values = tok[q].reshape(rows, parts * depth)
        at = pl.ds(2 * q, 2)
        total = jnp.dot(values, bd_ref[...], preferred_element_type=F32)
        bc_ref[at] = total[:, : 2 * state_size].astype(BF16).reshape(2, slots, 2 * state_size)
        prepare(q, total[:, 2 * state_size :])
        total = jnp.dot(values, x_ref[...], preferred_element_type=F32)
        xs_ref[at] = total.astype(BF16).reshape(2, slots, inner)

    def project_gates(q):
        values = tok[q].reshape(rows, parts * depth)
        total = jnp.dot(values, z_ref[...], preferred_element_type=F32)
        zs_ref[pl.ds(2 * q, 2)] = total.astype(BF16).reshape(2, slots, inner)

    def reached(q):
        return jnp.where(q < lag, 0, jnp.minimum(2 * (q - lag + 1), q + 1))

    def round_trip(q, carry):
        far_copy(q).wait_recv()
        diag_copy(q).start()

        @pl.when(q + ahead < rounds)
        def _():
            far_copy(q + ahead).start()

        @pl.when(q == 1)
        def _():
            piece_copy().wait_recv()
            across_copy(group, low).start()
            pass_copy(group, low).start()
            relay_start(1)

        for step in range(1, share):

            @pl.when(q == min(1 + 2 * step, rounds - 1))
            def _():
                relay_take(step)
                if step + 1 < share:
                    relay_start(step + 1)

        @pl.when(q == rounds - 2)
        def _():
            for j in range(chunks // 2):
                norm_copy(2, j).start()
                norm_copy(3, j).start()

        project(q)

        @pl.when(q == lag)
        def _():
            for k in range(1, shards):
                store_copy(k).wait_recv()

        @pl.loop(reached(q - 1), reached(q))
        def _(done):
            states(done, 0)
            states(done, 1)

        @pl.when(q == rounds - 1)
        def _():
            for k in range(1, shards):
                for c in range(capacity):
                    outgoing[k * capacity + c] = state_ref[look(3, k * capacity + c, sessions)]
            for k in range(1, shards):
                back_copy(k, 0).start()

        project_gates(q)

        @pl.loop(reached(q - 1), reached(q))
        def _(done):
            outputs(done, 0)
            outputs(done, 1)

        return carry

    lax.fori_loop(0, rounds, round_trip, 0)

    for j in range(chunks):
        norm_copy(1, j).start()
    for j in range(chunks // 2, chunks):
        norm_copy(2, j).start()
        norm_copy(3, j).start()
    for c in range(capacity):
        for n in range(2):
            there = slice(n * tail, (n + 1) * tail)
            returned[n][c] = state_ref[look(3, c, sessions), there, :]

    whole_copy().wait_recv()
    for j in range(chunks):
        norm_copy(1, j).wait_recv()

    @pl.loop(0, model // tile)
    def _(t):
        cols = pl.ds(pl.multiple_of(t * tile, tile), tile)
        mine = jnp.concatenate([normed[2 * (chunks + j) + half] for j in range(chunks)], axis=0)
        total = jnp.dot(mine, outw[0, :, cols], preferred_element_type=F32)
        theirs = got[0].reshape(chunks * slots, inner)
        total += jnp.dot(theirs, outw[1, :, cols], preferred_element_type=F32)
        sums[:, :, cols] = total.reshape(chunks, slots, tile)

    for k in range(1, shards):
        back_copy(k, 1).start()
    for j in range(chunks // 2):
        norm_copy(2, j).wait_send()
        norm_copy(3, j).wait_send()
    for k in range(share):
        across_copy(1 - group, k).wait_recv()
        pass_copy(1 - group, k).start()
    for k in range(share):
        for g in range(2):
            pass_copy(g, k).wait_recv()

    for n in range(2):
        span = slice(n * chunks // 2, (n + 1) * chunks // 2)
        for j in range(span.start, span.stop):
            norm_copy(2, j).wait_recv()
            norm_copy(3, j).wait_recv()

        @pl.loop(0, model // tile)
        def _(t):
            cols = pl.ds(pl.multiple_of(t * tile, tile), tile)
            total = sums[span, :, cols].reshape(chunks // 2 * slots, tile)
            for s in (2, 3):
                total += jnp.dot(
                    got[s - 1, span].reshape(chunks // 2 * slots, inner),
                    outw[s, :, cols],
                    preferred_element_type=F32,
                )
            out_ref[span.start * slots : span.stop * slots, cols] = total.astype(BF16)

        for k in range(1, shards):
            back_copy(k, n).wait_recv()

        where = [look(1, r, shards * capacity) for r in range(sessions)]

        @pl.loop(0, blocks // 4)
        def _(b):
            def stack(b):
                at = pl.ds(pl.multiple_of(b * band, band), band)
                return jnp.concatenate([returned[n][spot, at, :] for spot in where], axis=0)

            found = jnp.concatenate([stack(2 * b), stack(2 * b + 1)], axis=1)
            moved = jnp.dot(swap_out, found, preferred_element_type=F32).astype(BF16)
            for m in range(2):
                base = (n * (blocks // 2) + 2 * b + m) * (band * 128)
                for a in range(band):
                    new_store_ref[:, pl.ds(pl.multiple_of(base + a * 128, 128), 128)] = moved[
                        a * sessions : (a + 1) * sessions, m * 128 : (m + 1) * 128
                    ]

    @pl.loop(0, rounds)
    def _(q):
        far_copy(q).wait_send()
        sib_copy(q).wait_send()
        diag_copy(q).wait_send()

    for j in range(chunks):
        norm_copy(1, j).wait_send()
    for j in range(chunks // 2, chunks):
        norm_copy(2, j).wait_send()
        norm_copy(3, j).wait_send()
    for k in range(1, shards):
        store_copy(k).wait_send()
        for n in range(2):
            back_copy(k, n).wait_send()
    piece_copy().wait_send()
    whole_copy().wait_send()
    for k in range(share):
        across_copy(group, k).wait_send()
        for g in range(2):
            pass_copy(g, k).wait_send()
    for step in range(1, share):
        for way in (1, -1):

            @pl.when(relay_sends(way, step))
            def _():
                relay_copy(way, step).wait_send()


def run_layer(counts, home, tokens4, store, weights, params, out_weight, sizes, shards, capacity):
    heads, head_size, state_size = sizes
    parts, chunks, slots, depth = tokens4.shape
    x_weight, z_weight, bc_weight, dt_weight = weights
    inner = heads * head_size
    model = out_weight.shape[1]
    sessions, state_width = store.shape
    share = min(4, shards)
    pieces = 2 * share
    rounds = 2 * chunks
    vmem = pl.BlockSpec(memory_space=pltpu.VMEM)
    hbm = pl.BlockSpec(memory_space=pl.ANY)
    dma = pltpu.SemaphoreType.DMA
    state = (state_width // 128, 128)
    exchange = pltpu.VMEM((shards * capacity,) + state, BF16)
    piece = pltpu.VMEM((shards * capacity, state[0] // 2, state[1]), BF16)
    kept = pltpu.VMEM((sessions,) + state, BF16)
    width = parts * depth
    return pl.pallas_call(
        functools.partial(
            layer_kernel, heads, head_size, state_size, chunks, parts, shards, share, capacity
        ),
        out_shape=(
            pltpu.VMEM((chunks * slots, model), BF16),
            pltpu.VMEM(store.shape, BF16),
        ),
        in_specs=[pl.BlockSpec(memory_space=pltpu.SMEM)] + [hbm] * 6 + [vmem] * 4 + [hbm],
        out_specs=(vmem, vmem),
        scratch_shapes=[
            pltpu.VMEM((width, inner), BF16),
            pltpu.VMEM((width, inner), BF16),
            pltpu.VMEM((width, 2 * state_size + 128), BF16),
            pltpu.VMEM((parts, inner, model), BF16),
            pltpu.VMEM((rounds, 2, slots, width), BF16),
            pltpu.VMEM(home.shape, jnp.int32),
            pltpu.VMEM((8, 128), jnp.int32),
            pltpu.SMEM((8, 128), jnp.int32),
            pltpu.VMEM(store.shape, BF16),
            kept,
            exchange,
            exchange,
            kept,
            exchange,
            piece,
            piece,
            pltpu.VMEM((sessions, slots, inner), BF16),
            pltpu.VMEM((sessions, slots, inner), BF16),
            pltpu.VMEM((sessions, slots, 2 * state_size), BF16),
            pltpu.VMEM((sessions, 4 * heads, slots), F32),
            pltpu.VMEM((sessions, slots, 128), BF16),
            pltpu.VMEM((128, heads * 128 + inner), BF16),
            pltpu.VMEM((sessions, slots, inner), BF16),
            pltpu.VMEM((parts - 1, chunks, slots, inner), BF16),
            pltpu.VMEM((chunks, slots, model), F32),
            dma((3 + 3 * parts,)),
            dma,
        ]
        + [dma((rounds,))] * 7
        + [dma((shards,))] * 2
        + [dma((shards, 2))] * 2
        + [dma, dma]
        + [dma((2 * share,))] * 2
        + [dma((share,))] * 2
        + [dma((pieces + 1,))] * 2
        + [dma((parts - 1, chunks))] * 2,
        compiler_params=pltpu.CompilerParams(
            vmem_limit_bytes=56 * 1024 * 1024, collective_id=0, has_side_effects=True
        ),
        cost_estimate=pl.CostEstimate(
            flops=2 * sessions * slots * width * (2 * inner + 256 + model // parts),
            bytes_accessed=16 * 1024 * 1024,
            transcendentals=sessions * slots * heads * slots,
        ),
        name="layer",
    )(
        counts,
        home,
        tokens4,
        store,
        x_weight,
        z_weight,
        bc_weight,
        dt_weight.T,
        *params,
        out_weight,
    )


def body(
    tokens,
    x_weight,
    z_weight,
    bc_weight,
    dt_weight,
    dt_bias,
    decay_rate,
    norm_gain,
    out_weight,
    store_states,
    home_rows,
    event_counts,
):
    shards = lax.axis_size("dp")
    parts = lax.axis_size("mp")
    sessions = store_states.shape[0]
    capacity = max(2, (sessions + shards - 1) // shards)
    heads = dt_bias.shape[0]
    inner = x_weight.shape[1]
    state_size = bc_weight.shape[1] // 2
    slots = tokens.shape[0] // sessions
    tokens4 = tokens.reshape(parts, sessions // parts, slots, tokens.shape[1])
    return run_layer(
        event_counts,
        home_rows[None, :],
        tokens4,
        store_states,
        (x_weight, z_weight, bc_weight, dt_weight),
        (dt_bias[None, :], decay_rate[None, :], norm_gain[None, :]),
        out_weight,
        (heads, inner // heads, state_size),
        shards,
        capacity,
    )


def solution(mesh):
    return jax.shard_map(
        body,
        mesh=mesh,
        in_specs=(
            P(("groups", "dp"), "mp"),
            P(None, "mp"),
            P(None, "mp"),
            P(None, "mp"),
            P(None, "mp"),
            P("mp"),
            P("mp"),
            P("mp"),
            P("mp", None),
            P(("groups", "dp"), "mp"),
            P("groups"),
            P(("groups", "dp")),
        ),
        out_specs=(P(("groups", "dp", "mp"), None), P(("groups", "dp"), "mp")),
        check_vma=False,
    )
```
